32 devices in a mesh: dp: 4 (over y, x), tensor: 2 (over core), expert: 4 (over z).
Axes of the slice: x: 2, y: 2, z: 4, core: 2. Of those that a mesh axis runs over, the one named last changes fastest.
Arguments:
- tokens: bfloat16 [2048, 2304], P(('dp', 'tensor', 'expert')), may hold values from -6 to 6
- routes: int32 [2048, 2], P(('dp', 'tensor', 'expert')), may hold values from 0 to 7, all different within a row; in each aligned block of 64 rows (0 to 63, 64 to 127, ...) at most 24 rows name the same one
- gates: float32 [2048, 2], P(('dp', 'tensor', 'expert')), may hold values from 0.2 to 1
- segments: int32 [2048], P(('dp', 'tensor', 'expert')), may hold values from 0 to 7, never falling along the last dimension, each value on 1 to 512 neighbouring positions
- w_gate: bfloat16 [8, 2304, 7680], P('expert', None, ('dp', 'tensor')), may hold values from -0.125 to 0.125
- w_up: bfloat16 [8, 2304, 7680], P('expert', None, ('dp', 'tensor')), may hold values from -0.125 to 0.125
- w_down: bfloat16 [8, 7680, 2304], P('expert', ('dp', 'tensor')), may hold values from -0.0625 to 0.0625
Outputs:
- embedded: bfloat16 [2048, 2304], P(('dp', 'tensor', 'expert'))
- pooled: float32 [8, 2304], replicated
The draws below stay inside these ranges and needn't reach their ends.
Inputs may be any that keep to these rules, and one draw needn't show every extreme that they name: `routes`: each residue names two different experts. Within the rows of one device no expert is named more than 24 times, and in every draw some expert is named exactly 24 times by the rows of some device. `segments`: sequence numbers never fall along the residues; each sequence has 1 to 512 residues and one has exactly 512.
All inputs are finite; a program needn't handle non-finite values.
Results may differ from the reference program's by a relative error of at most 0.0085.
Values may be sent and summed in bfloat16 or wider, within the bound.
No kernel may reach another device: no remote copies, remote signals or barrier semaphores. Data moves between devices by JAX's collectives and lax.ppermute only.
A program may use at most 128 MiB of HBM per device.

```python
import math
import jax
import jax.numpy as jnp
import numpy as np
from jax import lax

D = 2304
FF = 7680
EXPERTS = 8
TOP = 2
TOK_DEV = 64
SEQ_MAX = 512
CAP = 24
REPL = 1
SLOTS = 8
FF_SLOT = 7680
WSH = 8
FF_DEV = 960
TOKENS = 2048
NSEQ = 8


def levels(rng, dims, shards, smallest, largest):
    gain = 1.0
    for dim, blocks in shards:
        steps = jax.random.uniform(jax.random.fold_in(jax.random.fold_in(rng, 6), dim), (blocks,), jnp.float32, smallest / len(shards), largest / len(shards))
        gain = gain * jnp.repeat(jnp.exp(steps), dims[dim] // blocks).reshape((-1,) + (1,) * (len(dims) - 1 - dim))
    return gain


def length_profile(count, total, bound, lean):
    weights = [(1 << 20) // math.isqrt(rank ** lean) + 1 for rank in range(2, count + 1)]
    surplus, holding = total - bound - (count - 1), [1] * (count - 1)
    while surplus > 0:
        movable = [i for i in range(count - 1) if holding[i] < bound]
        mass, left = sum([weights[i] for i in movable]), surplus
        for i in movable:
            addition = min(bound - holding[i], max(1, left * weights[i] // mass), surplus)
            holding[i] = holding[i] + addition
            surplus = surplus - addition
    return np.array([bound] + holding)


def ragged(own_key, number_of, total, bound, skew):
    if number_of == 2:
        one = jax.random.randint(own_key, (), max(1, total - bound), min(bound, total - 1) + 1)
        return jnp.stack([one, total - one])
    lengths = jnp.asarray(length_profile(number_of, total, bound, skew), jnp.int32)
    pairs = (number_of - 1) // 2
    source_of, taker = lengths[1:1 + 2 * pairs:2], lengths[2:2 + 2 * pairs:2]
    margin = jnp.minimum(source_of - 1, bound - taker)
    passed = jax.random.randint(jax.random.fold_in(own_key, 1), (pairs,), 0, 1 << 20) % (margin + 1)
    lengths = lengths.at[1:1 + 2 * pairs:2].set(source_of - passed).at[2:2 + 2 * pairs:2].set(taker + passed)
    return lengths[jax.random.permutation(jax.random.fold_in(own_key, 2), number_of)]


def deal_out(rng, own, number, rows, count, top, most, slope):
    sequence = jax.random.permutation(rng, count)
    packed, common = portions_of(count, rows * top, most, slope, True), portions_of(count, rows * top, most, slope, False)
    places = jnp.arange(count)

    def named(tallies, turn):
        used = int((tallies > 0).sum())
        fixed = max(1, used // 4)
        moved = fixed + (places - fixed + turn * (used - fixed)) % max(1, count - fixed)
        return jnp.zeros((count,), jnp.int32).at[sequence[jnp.where(places < fixed, places, moved)]].set(jnp.asarray(tallies, jnp.int32))

    tallies = jnp.where(number % 4 == 0, named(packed, number // 4), named(common, number - number // 4 - 1))
    mixed = jax.random.permutation(jax.random.fold_in(own, 3), count)
    giver, receiver = mixed[0:count // 2 * 2:2], mixed[1:count // 2 * 2:2]
    room = jnp.minimum(tallies[giver] - 1, most - tallies[receiver]) // 2
    room = jnp.where((giver == sequence[0]) | (receiver == sequence[0]) | (tallies[receiver] == 0), 0, jnp.maximum(room, 0))
    moved = jax.random.randint(jax.random.fold_in(own, 4), (count // 2,), 0, 1 << 20) % (room + 1)
    tallies = tallies.at[giver].add(-moved).at[receiver].add(moved)
    labels = jnp.searchsorted(jnp.cumsum(tallies), jnp.arange(rows * top), side="right").astype(jnp.int32)
    table = labels.reshape(top, rows).T
    table = table[jax.random.permutation(jax.random.fold_in(own, 1), rows)]
    turn = jax.random.randint(jax.random.fold_in(own, 2), (rows, 1), 0, top)
    return jnp.take_along_axis(table, (jnp.arange(top)[None, :] + turn) % top, axis=1)


def portions_of(count, total, reach, slope, full):
    weights = [(1 << 20) // math.isqrt(rank ** slope) + 1 for rank in range(1, count + 1)]
    largest = reach if full else min(reach, max(-(-total // count), total * weights[0] // sum(weights)))
    least = 1 if total - largest >= count - 1 else 0
    given, spare = [largest] + [least] * (count - 1), total - largest - least * (count - 1)
    while spare > 0:
        movable = [i for i in range(1, count) if given[i] < largest] or [i for i in range(1, count) if given[i] < reach]
        pool, remaining = sum([weights[i] for i in movable]), spare
        for i in movable:
            more = min(reach - given[i], max(1, remaining * weights[i] // pool), spare)
            given[i] = given[i] + more
            spare = spare - more
    return np.array(given)


def gaussian(stream_key, dims, deviation, reach, pieces=(), kind=jnp.bfloat16):
    result = deviation * jax.random.normal(stream_key, dims, jnp.float32)
    if pieces:
        result = result * levels(stream_key, dims, pieces, -0.22, 0.18)
    return jnp.clip(result, -reach, reach).astype(kind)


def setup_inputs(seed: int = 0) -> dict:
    key_list = jax.random.split(jax.random.key(seed), 8)
    tokens = gaussian(key_list[0], (TOKENS, D), 1.0, 6.0, ((0, 32),))
    routes_keys = jax.random.split(jax.random.fold_in(key_list[1], 1), TOKENS // TOK_DEV)
    routes_turns = jax.random.permutation(jax.random.fold_in(key_list[1], 3), TOKENS // TOK_DEV)
    routes = jax.vmap(lambda own, number: deal_out(jax.random.fold_in(key_list[1], 2), own, number, TOK_DEV, EXPERTS, TOP, CAP, 2))(routes_keys, routes_turns).reshape((TOKENS, TOP))
    gates = jnp.clip(0.2 + 0.8 * jax.random.uniform(key_list[2], (TOKENS, TOP), jnp.float32) ** levels(key_list[2], (TOKENS, TOP), ((0, 32),), -0.2, 0.2), 0.2, 1.0)
    segments = jnp.searchsorted(jnp.cumsum(ragged(key_list[3], NSEQ, TOKENS, SEQ_MAX, 2)), jnp.arange(TOKENS), side="right").astype(jnp.int32)
    w_gate = gaussian(key_list[4], (SLOTS, D, FF_SLOT), D ** -0.5, 0.125, ((0, 4), (2, 8)))
    w_up = gaussian(key_list[5], (SLOTS, D, FF_SLOT), D ** -0.5, 0.125, ((0, 4), (2, 8)))
    w_down = gaussian(key_list[6], (SLOTS, FF_SLOT, D), FF ** -0.5, 0.0625, ((0, 4), (1, 8)))
    return {"tokens": tokens, "routes": routes, "gates": gates, "segments": segments, "w_gate": w_gate, "w_up": w_up, "w_down": w_down}


epsilon = 1e-06

def reference(tokens, routes, gates, segments, w_gate, w_up, w_down):
    values = tokens.astype(jnp.float32)
    normed = (values * lax.rsqrt(lax.optimization_barrier(jnp.mean(values * values, axis=1, keepdims=True)) + epsilon)).astype(jnp.bfloat16)
    blocks = TOKENS // TOK_DEV
    flat_routes = routes.reshape(blocks, TOK_DEV * TOP)
    onehot = (flat_routes[:, :, None] == jnp.arange(EXPERTS, dtype=jnp.int32)[None, None, :]).astype(jnp.int32)
    slot_rank = lax.optimization_barrier(jnp.sum((jnp.cumsum(onehot, axis=1) - onehot) * onehot, axis=2))
    block_index = jnp.arange(blocks, dtype=jnp.int32)[:, None]
    slot_index = ((block_index * EXPERTS + flat_routes) * CAP + slot_rank).reshape(-1).astype(jnp.int32)
    source = jnp.repeat(normed, TOP, axis=0)
    buffer = jnp.zeros((blocks * EXPERTS * CAP, D), jnp.bfloat16).at[slot_index].set(source)
    by_expert = buffer.reshape(blocks, EXPERTS, CAP, D).transpose(1, 0, 2, 3).reshape(EXPERTS, blocks * CAP, D)
    gate_full = w_gate.reshape(EXPERTS, REPL, D, FF_SLOT).transpose(0, 2, 1, 3).reshape(EXPERTS, D, FF)
    up_full = w_up.reshape(EXPERTS, REPL, D, FF_SLOT).transpose(0, 2, 1, 3).reshape(EXPERTS, D, FF)
    down_full = w_down.reshape(EXPERTS, FF, D)

    def one_expert(operands):
        row_block, gate_weight, up_weight, down_weight = operands
        gate_proj = jnp.dot(row_block, gate_weight, preferred_element_type=jnp.float32)
        up_proj = jnp.dot(row_block, up_weight, preferred_element_type=jnp.float32)
        hidden = (jax.nn.silu(gate_proj) * up_proj).astype(jnp.bfloat16)
        partials = jnp.einsum('rkf,kfd->krd', hidden.reshape(-1, REPL * WSH, FF_DEV).astype(jnp.float32), down_weight.reshape(REPL * WSH, FF_DEV, D).astype(jnp.float32))
        partials = lax.optimization_barrier(partials.astype(jnp.bfloat16)).astype(jnp.float32)
        group_out = partials.reshape(REPL, WSH, -1, D).sum(axis=1)
        group_out = lax.optimization_barrier(group_out.astype(jnp.bfloat16)).astype(jnp.float32)
        return group_out.sum(axis=0)
    expert_out = lax.map(one_expert, (by_expert, gate_full, up_full, down_full))
    out_flat = expert_out.reshape(EXPERTS, blocks, CAP, D).transpose(1, 0, 2, 3).reshape(-1, D)
    picked = out_flat[slot_index].reshape(TOKENS, TOP, D)
    mixed = values + lax.optimization_barrier(jnp.sum(gates[:, :, None] * picked, axis=1))
    embedded = mixed.astype(jnp.bfloat16)
    seq_hot = (jnp.arange(NSEQ, dtype=jnp.int32)[:, None] == segments[None, :]).astype(jnp.bfloat16)
    seq_sums = jnp.dot(seq_hot, embedded, preferred_element_type=jnp.float32)
    seq_counts = lax.optimization_barrier(jnp.sum(seq_hot.astype(jnp.float32), axis=1))
    pooled = seq_sums / seq_counts[:, None]
    return (embedded, pooled)
```

```python
import functools

import jax
import jax.numpy as jnp
from jax import lax
from jax.experimental import pallas as pl
from jax.experimental.pallas import tpu as pltpu
from jax.sharding import PartitionSpec as P

EXPERTS = 8
TOP = 2
CAP = 24
LANES = 128
AXES = ("dp", "tensor", "expert")


epsilon = 1e-06


def xor_steps(size):
    return size & (size - 1) == 0


def swap(x, d=0, t=0, z=0, turned=None):
    sizes = [lax.axis_size(name) for name in AXES]
    pairs = []
    for i in range(sizes[0]):
        for j in range(sizes[1]):
            for k in range(sizes[2]):
                flip = d if turned is None or j % 2 == 0 else turned
                here = (i * sizes[1] + j) * sizes[2] + k
                there = ((i ^ flip) * sizes[1] + (j ^ t)) * sizes[2] + (k ^ z)
                pairs.append((here, there))
    return lax.ppermute(x, AXES, pairs)


def prep_kernel(seqs, planes, pos, tokens, routes, gates, seg_row, seg_col, own, other, weights, sums):
    tok_count, width = tokens.shape
    slots = 2 * planes * CAP
    t, z = pos[0], pos[1]
    raw = tokens[...]
    values = raw.astype(jnp.float32)
    scale = lax.rsqrt(jnp.mean(values * values, axis=1, keepdims=True) + epsilon)
    normed = (values * scale).astype(jnp.bfloat16)

    expert = lax.broadcasted_iota(jnp.int32, (EXPERTS, tok_count), 0)
    hot = [expert == routes[k : k + 1, :] for k in range(TOP)]
    named = (hot[0] | hot[1]).astype(jnp.bfloat16)
    earlier = (
        lax.broadcasted_iota(jnp.int32, (tok_count, tok_count), 0)
        < lax.broadcasted_iota(jnp.int32, (tok_count, tok_count), 1)
    ).astype(jnp.bfloat16)
    before = jnp.dot(named, earlier, preferred_element_type=jnp.float32)

    row = lax.broadcasted_iota(jnp.int32, (slots, tok_count), 0)
    group = row // CAP
    rank = row - group * CAP
    row_expert = 2 * (z ^ (group % planes)) + (t ^ (group // planes))
    place = jnp.zeros((slots, tok_count), jnp.float32)
    weight = jnp.zeros((slots, tok_count), jnp.float32)
    for k in range(TOP):
        own_rank = jnp.sum(jnp.where(hot[k], before, 0.0), axis=0, keepdims=True).astype(jnp.int32)
        hit = (row_expert == routes[k : k + 1, :]) & (rank == own_rank)
        place = place + jnp.where(hit, 1.0, 0.0)
        weight = weight + jnp.where(hit, gates[k : k + 1, :], 0.0)
    weights[...] = weight

    rows = jnp.dot(place.astype(jnp.bfloat16), normed, preferred_element_type=jnp.float32).astype(jnp.bfloat16)
    high = weight.astype(jnp.bfloat16)
    low = (weight - high.astype(jnp.float32)).astype(jnp.bfloat16)
    lane = lax.broadcasted_iota(jnp.int32, (tok_count, LANES), 1)
    member = (lane == seg_col[...]).astype(jnp.bfloat16)
    member_low = (lane == seg_col[...] + seqs).astype(jnp.bfloat16)
    marks = (
        jnp.dot(high, member, preferred_element_type=jnp.float32)
        + jnp.dot(low, member_low, preferred_element_type=jnp.float32)
    ).astype(jnp.bfloat16)
    half = planes * CAP
    own[:, :width] = rows[:half]
    own[:, width:] = marks[:half]
    other[:, :width] = rows[half:]
    other[:, width:] = marks[half:]

    seq_hot = lax.broadcasted_iota(jnp.int32, (seqs, tok_count), 0) == seg_row[...]
    sums[:, :width] = jnp.dot(seq_hot.astype(jnp.bfloat16), raw, preferred_element_type=jnp.float32)
    counts = jnp.sum(seq_hot.astype(jnp.float32), axis=1, keepdims=True)
    sums[:, width:] = jnp.broadcast_to(counts, (seqs, LANES))


def prep(pos, tokens, routes, gates, segments, seqs, planes):
    tok_count, width = tokens.shape
    half = planes * CAP
    vmem = pl.BlockSpec(memory_space=pltpu.VMEM)
    return pl.pallas_call(
        functools.partial(prep_kernel, seqs, planes),
        out_shape=(
            jax.ShapeDtypeStruct((half, width + LANES), jnp.bfloat16),
            jax.ShapeDtypeStruct((half, width + LANES), jnp.bfloat16),
            jax.ShapeDtypeStruct((2 * half, tok_count), jnp.float32),
            jax.ShapeDtypeStruct((seqs, width + LANES), jnp.float32),
        ),
        in_specs=[pl.BlockSpec(memory_space=pltpu.SMEM)] + [vmem] * 5,
        out_specs=(vmem,) * 4,
        name="prep",
    )(pos, tokens, routes.T, gates.T, segments[None, :], segments[:, None])


def ffn_kernel(pieces, tile, cols, pos, *refs):
    parts = refs[:pieces]
    gate_own, up_own, down_own, gate_far, up_far, down_far = refs[pieces : pieces + 6]
    outs = refs[pieces + 6 : 2 * pieces + 6]
    rows_buf, gate_buf, up_buf, down_buf, hidden, row_sem, in_sem, out_sem = refs[2 * pieces + 6 :]
    t = pos[0]
    size, width = parts[0].shape
    units = down_far.shape[0]
    row_copies = [
        pltpu.make_async_copy(parts[i], rows_buf.at[pl.ds(i * size, size)], row_sem.at[i]) for i in range(pieces)
    ]
    for copy in row_copies:
        copy.start()
    sources = [(gate_own.at[t], up_own.at[t], down_own.at[t]), (gate_far, up_far, down_far)]
    spans = [(start, min(tile, units - start)) for start in range(0, units, tile)]
    in_copies = []
    for h in range(2):
        for j, (start, length) in enumerate(spans):
            here = pl.ds(start, length)
            pair = [
                pltpu.make_async_copy(sources[h][m].at[here], buf.at[h, here], in_sem.at[m, h * len(spans) + j])
                for m, buf in enumerate((gate_buf, up_buf))
            ]
            for copy in pair:
                copy.start()
            in_copies.append(pair)
    down_copies = []
    for h in range(2):
        copy = pltpu.make_async_copy(sources[h][2], down_buf.at[pl.ds(h * units, units)], out_sem.at[h])
        copy.start()
        down_copies.append(copy)
    for copy in row_copies:
        copy.wait()
    x = rows_buf[...]
    nt = (((1,), (1,)), ((), ()))
    for h in range(2):
        for j, (start, length) in enumerate(spans):
            for copy in in_copies[h * len(spans) + j]:
                copy.wait()
            here = pl.ds(start, length)
            g = lax.dot_general(x, gate_buf[h, here], nt, preferred_element_type=jnp.float32)
            u = lax.dot_general(x, up_buf[h, here], nt, preferred_element_type=jnp.float32)
            value = g / (1.0 + jnp.exp(-g)) * u
            hidden[:, h * units + start : h * units + start + length] = value.astype(jnp.bfloat16)
    for copy in down_copies:
        copy.wait()
    for start in range(0, width, cols):
        length = min(cols, width - start)
        y = jnp.dot(hidden[...], down_buf[:, start : start + length], preferred_element_type=jnp.float32)
        for i in range(pieces):
            outs[i][:, start : start + length] = y[i * size : (i + 1) * size].astype(jnp.bfloat16)


def ffn(pos, parts, weights):
    pieces = len(parts)
    size, width = parts[0].shape
    units = weights[5].shape[0]
    tile, cols = 320, 768
    tiles = 2 * -(-units // tile)
    anywhere = pl.BlockSpec(memory_space=pl.ANY)
    vmem = pl.BlockSpec(memory_space=pltpu.VMEM)
    return pl.pallas_call(
        functools.partial(ffn_kernel, pieces, tile, cols),
        out_shape=(jax.ShapeDtypeStruct((size, width), jnp.bfloat16),) * pieces,
        in_specs=[pl.BlockSpec(memory_space=pltpu.SMEM)] + [anywhere] * (pieces + 6),
        out_specs=(vmem,) * pieces,
        scratch_shapes=[
            pltpu.VMEM((pieces * size, width), jnp.bfloat16),
            pltpu.VMEM((2, units, width), jnp.bfloat16),
            pltpu.VMEM((2, units, width), jnp.bfloat16),
            pltpu.VMEM((2 * units, width), jnp.bfloat16),
            pltpu.VMEM((pieces * size, 2 * units), jnp.bfloat16),
            pltpu.SemaphoreType.DMA((pieces,)),
            pltpu.SemaphoreType.DMA((2, tiles)),
            pltpu.SemaphoreType.DMA((2,)),
        ],
        compiler_params=pltpu.CompilerParams(vmem_limit_bytes=44 << 20),
        cost_estimate=pl.CostEstimate(
            flops=12 * pieces * size * width * units, transcendentals=2 * pieces * size * units,
            bytes_accessed=12 * units * width,
        ),
        name="ffn",
    )(pos, *parts, *weights)


def combine_kernel(tokens, first, second, weights, out):
    weight = weights[...].T
    high = weight.astype(jnp.bfloat16)
    low = (weight - high.astype(jnp.float32)).astype(jnp.bfloat16)
    half = first.shape[0]
    total = tokens[...].astype(jnp.float32)
    mixed = jnp.zeros_like(total)
    for part in (low, high):
        mixed = mixed + jnp.dot(part[:, :half], first[...], preferred_element_type=jnp.float32)
        mixed = mixed + jnp.dot(part[:, half:], second[...], preferred_element_type=jnp.float32)
    out[...] = (total + mixed).astype(jnp.bfloat16)


def combine(tokens, first, second, weights):
    vmem = pl.BlockSpec(memory_space=pltpu.VMEM)
    return pl.pallas_call(
        combine_kernel,
        out_shape=jax.ShapeDtypeStruct(tokens.shape, jnp.bfloat16),
        in_specs=[vmem] * 4,
        out_specs=vmem,
        name="combine",
    )(tokens, first, second, weights)


def added(*arrays):
    total = arrays[0].astype(jnp.float32)
    for array in arrays[1:]:
        total = total + array.astype(jnp.float32)
    return total.astype(jnp.bfloat16)


def core_shards(tokens, routes, gates, segments, w_gate, w_up, w_down):
    tok_count, width = tokens.shape
    planes = lax.axis_size("expert")
    devices_all = lax.axis_size("dp") * lax.axis_size("tensor") * planes
    seqs = tok_count * devices_all // 256
    t, z = lax.axis_index("tensor"), lax.axis_index("expert")
    pos = jnp.stack([t, z]).astype(jnp.int32)

    own, other, weights, sums = prep(pos, tokens, routes, gates, segments, seqs, planes)
    sibling = swap(other, t=1)

    stored = (jnp.swapaxes(w_gate, 1, 2), jnp.swapaxes(w_up, 1, 2), w_down)
    far = tuple(swap(lax.dynamic_index_in_dim(w, 1 - t, 0, keepdims=False), t=1) for w in stored)

    chunks = []
    for source in (own, sibling):
        blocks = [source[c * CAP : (c + 1) * CAP] for c in range(planes)]
        arrived = [blocks[0]] + [swap(blocks[c], z=c) for c in range(1, planes)]
        whole = jnp.concatenate(arrived, axis=0)
        rows, marks = whole[:, :width], whole[:, width:]
        near = swap(rows, d=1, turned=2)
        side = swap(rows, d=2, turned=1)
        across = swap(near, d=2, turned=1)
        chunks.append((marks, (rows, near, side, across)))

    returned = []
    pool = sums
    for marks, parts in chunks:
        mine, to_near, to_side, to_across = ffn(pos, parts, stored + far)
        passed = added(to_near, swap(to_across, d=2, turned=1))
        done = added(mine, swap(to_side, d=2, turned=1), swap(passed, d=1, turned=2))
        shares = lax.dot_general(
            marks[:, : 2 * seqs], done, (((0,), (0,)), ((), ())), preferred_element_type=jnp.float32
        )
        shares = shares[:seqs] + shares[seqs:]
        pool = pool + jnp.pad(shares, ((0, 0), (0, LANES)))
        blocks = [done[c * CAP : (c + 1) * CAP] for c in range(planes)]
        back = [blocks[0]] + [swap(blocks[c], z=c) for c in range(1, planes)]
        returned.append(jnp.concatenate(back, axis=0))

    second = swap(returned[1], t=1)
    embedded = combine(tokens, returned[0], second, weights)

    pool = pool + swap(pool, t=1)
    for axis in ("d", "z"):
        step = 1
        while step < lax.axis_size({"d": "dp", "z": "expert"}[axis]):
            pool = pool + swap(pool, **{axis: step})
            step *= 2
    pooled = pool[:, :width] / pool[:, width : width + 1]
    return (embedded, pooled)


def slot_numbers(routes):
    flat_routes = routes.reshape(-1)
    pairs = flat_routes.shape[0]
    same = flat_routes[:, None] == flat_routes[None, :]
    earlier = jnp.arange(pairs)[None, :] < jnp.arange(pairs)[:, None]
    slot_rank = jnp.sum((same & earlier).astype(jnp.int32), axis=1)
    return flat_routes * CAP + slot_rank


def shards(tokens, routes, gates, segments, w_gate, w_up, w_down):
    tok_count, width = tokens.shape
    experts_axis = lax.axis_size("expert")
    per_device = w_gate.shape[0]
    replicas = max(1, experts_axis // EXPERTS)
    plane = lax.axis_size("dp") * lax.axis_size("tensor")
    values = tokens.astype(jnp.float32)
    scale = lax.rsqrt(jnp.mean(values * values, axis=1, keepdims=True) + epsilon)
    normed = (values * scale).astype(jnp.bfloat16)
    slot_index = slot_numbers(routes)
    hits = jnp.arange(EXPERTS * CAP, dtype=jnp.int32)[:, None] == slot_index[None, :]
    placing = jnp.sum(hits.astype(jnp.int32).reshape(EXPERTS * CAP, tok_count, TOP), axis=2)
    slot_rows = jnp.dot(placing.astype(jnp.bfloat16), normed, preferred_element_type=jnp.float32)
    shaped = slot_rows.astype(jnp.bfloat16).reshape(EXPERTS, CAP, width)
    if replicas > 1:
        shaped = jnp.repeat(shaped, replicas, axis=0)
    send_rows = shaped.reshape(EXPERTS * replicas * CAP, width)
    received = lax.all_to_all(send_rows, "expert", split_axis=0, concat_axis=0, tiled=True)
    local_rows = received.reshape(experts_axis, per_device, CAP, width)
    block = lax.all_gather(local_rows, ("dp", "tensor"), axis=0, tiled=True)
    gate_proj = jnp.einsum("nacd,adf->nacf", block, w_gate, preferred_element_type=jnp.float32)
    up_proj = jnp.einsum("nacd,adf->nacf", block, w_up, preferred_element_type=jnp.float32)
    hidden = (jax.nn.silu(gate_proj) * up_proj).astype(jnp.bfloat16)
    summed = lax.psum_scatter(
        jnp.einsum("nacf,afd->nacd", hidden, w_down, preferred_element_type=jnp.float32).astype(jnp.bfloat16),
        ("dp", "tensor"),
        scatter_dimension=0,
        tiled=True,
    )
    returned = lax.all_to_all(summed, "expert", split_axis=0, concat_axis=0, tiled=True).astype(jnp.float32)
    expert_out = jnp.sum(returned.reshape(EXPERTS, replicas, CAP, width), axis=1)
    picked = jnp.take(expert_out.reshape(EXPERTS * CAP, width), slot_index, axis=0).reshape(tok_count, TOP, width)
    embedded = (values + jnp.sum(gates[:, :, None] * picked, axis=1)).astype(jnp.bfloat16)
    seq_total = tok_count * plane * experts_axis // 256
    seq_hot = jnp.arange(seq_total, dtype=jnp.int32)[:, None] == segments[None, :]
    seq_sums = jnp.dot(seq_hot.astype(jnp.bfloat16), embedded, preferred_element_type=jnp.float32)
    seq_counts = jnp.sum(seq_hot.astype(jnp.float32), axis=1)
    total_sums, total_counts = lax.psum((seq_sums, seq_counts), AXES)
    return (embedded, total_sums / total_counts[:, None])


def solution(mesh):
    placed = (
        P(AXES, None),
        P(AXES, None),
        P(AXES, None),
        P(AXES),
        P("expert", None, ("dp", "tensor")),
        P("expert", None, ("dp", "tensor")),
        P("expert", ("dp", "tensor"), None),
    )
    dp, tensor, planes = (mesh.shape[name] for name in AXES)
    paired = dp == 4 and tensor == 2 and EXPERTS == tensor * planes and xor_steps(planes)
    return jax.shard_map(
        core_shards if paired else shards,
        mesh=mesh,
        in_specs=placed,
        out_specs=(P(AXES, None), P()),
        check_vma=False,
    )
```

```python
import functools

import jax
import jax.numpy as jnp
from jax import lax
from jax.experimental import pallas as pl
from jax.experimental.pallas import tpu as pltpu
from jax.sharding import PartitionSpec as P

EXPERTS = 8
TOP = 2
CAP = 24
LANES = 128
VMEM_LIMIT = 48 << 20
AXES = ("dp", "tensor", "expert")


epsilon = 1e-06


def xor_steps(size):
    return size & (size - 1) == 0


def swap(x, d=0, t=0, z=0, turned=None):
    sizes = [lax.axis_size(name) for name in AXES]
    pairs = []
    for i in range(sizes[0]):
        for j in range(sizes[1]):
            for k in range(sizes[2]):
                flip = d if turned is None or j % 2 == 0 else turned
                here = (i * sizes[1] + j) * sizes[2] + k
                there = ((i ^ flip) * sizes[1] + (j ^ t)) * sizes[2] + (k ^ z)
                pairs.append((here, there))
    return lax.ppermute(x, AXES, pairs)


def prep_kernel(seqs, planes, tokens, routes, gates, seg_row, own, own_home, other, other_home, weights, sums):
    tok_count, width = tokens.shape
    slots = 2 * (planes + 1) * CAP
    t, z = lax.axis_index("tensor"), lax.axis_index("expert")
    raw = tokens[...]
    values = raw.astype(jnp.float32)
    scale = lax.rsqrt(jnp.mean(values * values, axis=1, keepdims=True) + epsilon)
    normed = (values * scale).astype(jnp.bfloat16)

    expert = lax.broadcasted_iota(jnp.int32, (EXPERTS, tok_count), 0)
    hot = [expert == routes[k : k + 1, :] for k in range(TOP)]
    named = (hot[0] | hot[1]).astype(jnp.bfloat16)
    earlier = (
        lax.broadcasted_iota(jnp.int32, (tok_count, tok_count), 0)
        < lax.broadcasted_iota(jnp.int32, (tok_count, tok_count), 1)
    ).astype(jnp.bfloat16)
    before = jnp.dot(named, earlier, preferred_element_type=jnp.float32)

    row = lax.broadcasted_iota(jnp.int32, (slots, tok_count), 0)
    group = row // CAP
    rank = row - group * CAP
    side = group // (planes + 1)
    plane = group - side * (planes + 1)
    row_expert = 2 * jnp.where(plane == planes, z, jnp.where(plane == z, EXPERTS, plane)) + (t ^ side)
    place = jnp.zeros((slots, tok_count), jnp.float32)
    weight = jnp.zeros((slots, tok_count), jnp.float32)
    for k in range(TOP):
        own_rank = jnp.sum(jnp.where(hot[k], before, 0.0), axis=0, keepdims=True).astype(jnp.int32)
        hit = (row_expert == routes[k : k + 1, :]) & (rank == own_rank)
        place = place + jnp.where(hit, 1.0, 0.0)
        weight = weight + jnp.where(hit, gates[k : k + 1, :], 0.0)
    weights[...] = weight

    rows = jnp.dot(place.astype(jnp.bfloat16), normed, preferred_element_type=jnp.float32).astype(jnp.bfloat16)
    high = weight.astype(jnp.bfloat16)
    low = (weight - high.astype(jnp.float32)).astype(jnp.bfloat16)
    lane = lax.broadcasted_iota(jnp.int32, (LANES, tok_count), 0)
    nt = (((1,), (1,)), ((), ()))
    marks = jnp.zeros((slots, LANES), jnp.float32)
    for part, first in ((high, 0), (low, seqs)):
        member = (lane == seg_row[...] + first).astype(jnp.bfloat16)
        marks = marks + lax.dot_general(part, member, nt, preferred_element_type=jnp.float32)
    marks = marks.astype(jnp.bfloat16)
    start = 0
    for out in (own, own_home, other, other_home):
        stop = start + out.shape[0]
        out[:, :width] = rows[start:stop]
        out[:, width:] = marks[start:stop]
        start = stop

    seq_hot = lax.broadcasted_iota(jnp.int32, (seqs, tok_count), 0) == seg_row[...]
    sums[:, :width] = jnp.dot(seq_hot.astype(jnp.bfloat16), raw, preferred_element_type=jnp.float32)
    counts = jnp.sum(seq_hot.astype(jnp.float32), axis=1, keepdims=True)
    sums[:, width:] = jnp.broadcast_to(counts, (seqs, LANES))


def prep(tokens, routes, gates, segments, seqs, planes):
    tok_count, width = tokens.shape
    vmem = pl.BlockSpec(memory_space=pltpu.VMEM)
    blocks = [
        jax.ShapeDtypeStruct((count * CAP, width + LANES), jnp.bfloat16) for count in (planes, 1, planes, 1)
    ]
    return pl.pallas_call(
        functools.partial(prep_kernel, seqs, planes),
        out_shape=(
            *blocks,
            jax.ShapeDtypeStruct((2 * (planes + 1) * CAP, tok_count), jnp.float32),
            jax.ShapeDtypeStruct((seqs, width + LANES), jnp.float32),
        ),
        in_specs=[vmem] * 4,
        out_specs=(vmem,) * 6,
        name="prep",
    )(tokens, routes.T, gates.T, segments[None, :])


def spans_of(total, tile):
    return [(start, min(tile, total - start)) for start in range(0, total, tile)]


def tie(value, *before):
    return lax.optimization_barrier((value,) + before)[0]


def ffn_kernel(pieces, tile, cols, depth, seqs, pool_in, *refs):
    parts, weights, outs = refs[:pieces], refs[pieces : pieces + 6], refs[pieces + 6 : 2 * pieces + 6]
    pool_out, rows_buf, gate_buf, up_buf, down_buf, hidden, row_sem, in_sem, down_sem = refs[2 * pieces + 6 :]
    t = lax.axis_index("tensor")
    halves = [[w.at[t] for w in weights[:3]], [w.at[t] for w in weights[3:]]]
    size = parts[0].shape[0]
    _, units, width = weights[0].shape
    row_copies = [
        pltpu.make_async_copy(parts[i], rows_buf.at[i, pl.ds(0, size)], row_sem.at[i]) for i in range(pieces)
    ]
    padded = rows_buf.shape[1]
    if padded > size:
        for i in range(pieces):
            rows_buf[i, size:] = jnp.zeros((padded - size, rows_buf.shape[2]), rows_buf.dtype)
    spans = spans_of(units, tile)
    col_spans = spans_of(width, cols)
    copies = []
    for h in range(2):
        for j, (start, length) in enumerate(spans):
            here = pl.ds(start, length)
            copies.append(
                [
                    pltpu.make_async_copy(halves[h][m].at[here], buf.at[h, here], in_sem.at[m, h * len(spans) + j])
                    for m, buf in enumerate((gate_buf, up_buf))
                ]
            )
    for j, (start, length) in enumerate(col_spans):
        here = pl.ds(start, length)
        copies.append(
            [
                pltpu.make_async_copy(
                    halves[h][2].at[:, here], down_buf.at[pl.ds(h * units, units), here], down_sem.at[h, j]
                )
                for h in range(2)
            ]
        )
    for copy in row_copies:
        copy.start()
    for group in copies[:depth]:
        for copy in group:
            copy.start()

    def arrive(i):
        for copy in copies[i]:
            copy.wait()
        for group in copies[i + depth : i + depth + 1]:
            for copy in group:
                copy.start()

    for copy in row_copies:
        copy.wait()
    x = rows_buf[:, :, :width].reshape(pieces * padded, width)
    marks = rows_buf[:, :, width:].reshape(pieces * padded, LANES).astype(jnp.float32).T[: 2 * seqs].astype(jnp.bfloat16)
    nt = (((1,), (1,)), ((), ()))
    for h in range(2):
        for j, (start, length) in enumerate(spans):
            arrive(h * len(spans) + j)
            here = slice(start, start + length)
            g = lax.dot_general(x, gate_buf[h, here], nt, preferred_element_type=jnp.float32)
            u = lax.dot_general(x, up_buf[h, here], nt, preferred_element_type=jnp.float32)
            value = g / (1.0 + jnp.exp(-g)) * u
            hidden[:, h * units + start : h * units + start + length] = value.astype(jnp.bfloat16)
    pool_out[:, width:] = pool_in[:, width:]
    for j, (start, length) in enumerate(col_spans):
        arrive(2 * len(spans) + j)
        here = slice(start, start + length)
        y = jnp.dot(hidden[...], down_buf[:, here], preferred_element_type=jnp.float32).astype(jnp.bfloat16)
        share = jnp.dot(marks, y, preferred_element_type=jnp.float32)
        pool_out[:, here] = pool_in[:, here] + share[:seqs] + share[seqs:]
        for i in range(pieces):
            outs[i][:, here] = y[i * padded : i * padded + size]


def ffn(parts, weights, pool):
    pieces = len(parts)
    size = parts[0].shape[0]
    _, units, width = weights[0].shape
    tile, cols, depth = 256, 768, 3
    padded = -(-size // 16) * 16
    rows = pieces * padded
    anywhere = pl.BlockSpec(memory_space=pl.ANY)
    vmem = pl.BlockSpec(memory_space=pltpu.VMEM)
    return pl.pallas_call(
        functools.partial(ffn_kernel, pieces, tile, cols, depth, pool.shape[0]),
        out_shape=(jax.ShapeDtypeStruct((size, width), jnp.bfloat16),) * pieces
        + (jax.ShapeDtypeStruct(pool.shape, pool.dtype),),
        in_specs=[vmem] + [anywhere] * (pieces + 6),
        out_specs=(vmem,) * (pieces + 1),
        scratch_shapes=[
            pltpu.VMEM((pieces, padded, width + LANES), jnp.bfloat16),
            pltpu.VMEM((2, units, width), jnp.bfloat16),
            pltpu.VMEM((2, units, width), jnp.bfloat16),
            pltpu.VMEM((2 * units, width), jnp.bfloat16),
            pltpu.VMEM((rows, 2 * units), jnp.bfloat16),
            pltpu.SemaphoreType.DMA((pieces,)),
            pltpu.SemaphoreType.DMA((2, 2 * len(spans_of(units, tile)))),
            pltpu.SemaphoreType.DMA((2, len(spans_of(width, cols)))),
        ],
        compiler_params=pltpu.CompilerParams(vmem_limit_bytes=VMEM_LIMIT),
        cost_estimate=pl.CostEstimate(
            flops=12 * rows * width * units, transcendentals=2 * rows * units, bytes_accessed=12 * units * width
        ),
        name="ffn",
    )(pool, *parts, *weights)


def settle_kernel(planes, *refs):
    parts, out = refs[:-1], refs[-1]
    z = lax.axis_index("expert")
    total = parts[0][...].astype(jnp.float32)
    for part in parts[1:]:
        total = total + part[...].astype(jnp.float32)
    for j in range(planes - 1):
        out[lax.rem(z + 1 + j, planes)] = total[j * CAP : (j + 1) * CAP].astype(jnp.bfloat16)
    out[z] = jnp.zeros(out.shape[1:], jnp.bfloat16)


def settle(parts, planes):
    vmem = pl.BlockSpec(memory_space=pltpu.VMEM)
    return pl.pallas_call(
        functools.partial(settle_kernel, planes),
        out_shape=jax.ShapeDtypeStruct((planes, CAP, parts[0].shape[1]), jnp.bfloat16),
        in_specs=[vmem] * len(parts),
        out_specs=vmem,
        name="settle",
    )(*parts)


def combine_kernel(tokens, weights, *refs):
    parts, out = refs[:-1], refs[-1]
    mixed = jnp.zeros(tokens.shape, jnp.float32)
    start = 0
    for part in parts:
        stop = start + part.shape[0]
        weight = weights[start:stop].T
        high = weight.astype(jnp.bfloat16)
        low = (weight - high.astype(jnp.float32)).astype(jnp.bfloat16)
        for factor in (low, high):
            mixed = mixed + jnp.dot(factor, part[...], preferred_element_type=jnp.float32)
        start = stop
    out[...] = (tokens[...].astype(jnp.float32) + mixed).astype(jnp.bfloat16)


def combine(tokens, weights, parts):
    vmem = pl.BlockSpec(memory_space=pltpu.VMEM)
    return pl.pallas_call(
        combine_kernel,
        out_shape=jax.ShapeDtypeStruct(tokens.shape, jnp.bfloat16),
        in_specs=[vmem] * (2 + len(parts)),
        out_specs=vmem,
        name="combine",
    )(tokens, weights, *parts)


def added(*arrays):
    total = arrays[0].astype(jnp.float32)
    for array in arrays[1:]:
        total = total + array.astype(jnp.float32)
    return total.astype(jnp.bfloat16)


def core_shards(tokens, routes, gates, segments, w_gate, w_up, w_down):
    tok_count, width = tokens.shape
    chips, cores, planes = (lax.axis_size(name) for name in AXES)
    seqs = tok_count * chips * cores * planes // 256

    own, own_home, other, other_home, weights, pool = prep(tokens, routes, gates, segments, seqs, planes)
    sibling, sibling_home = swap(other, t=1), swap(other_home, t=1)
    stored = (jnp.swapaxes(w_gate, 1, 2), jnp.swapaxes(w_up, 1, 2), w_down)

    tied = lax.optimization_barrier(stored + (sibling,))
    far = tuple(pltpu.with_memory_space_constraint(swap(array, t=1), pltpu.HBM) for array in tied[:3])

    z = lax.axis_index("expert")
    others = (planes - 1) * CAP

    def exchange(rows):
        return lax.all_to_all(rows, "expert", split_axis=0, concat_axis=0, tiled=True)

    def outward(rows):
        return lax.dynamic_slice_in_dim(jnp.concatenate([rows, rows]), (z + 1) * CAP, others)

    def sent_on(arrays):
        return [swap(array, d=step, turned=turned) for array, (step, turned) in zip(arrays, ((1, 2), (2, 1), (3, 3)))]

    def together(arrays, *before):
        return list(lax.optimization_barrier(tuple(arrays) + before))[: len(arrays)]

    home = jnp.concatenate([own_home, sibling_home])
    arrived = exchange(own)
    home_near, home_side = swap(home, d=1, turned=2), swap(home, d=2, turned=1)
    arrived, home_near = together([arrived], home_near)[0], home_near
    early = outward(arrived)
    near, side = swap(early, d=1, turned=2), swap(early, d=2, turned=1)
    late = outward(exchange(tie(sibling, early)))
    first = [early, near, side, swap(near, d=2, turned=1)]
    home = [home, home_near, home_side, swap(home_near, d=2, turned=1)]
    second = [late] + sent_on([late] * 3)

    def back(parts):
        return [parts[0]] + sent_on(parts[1:])

    *partial, pool = ffn(first, stored + far, pool)
    early = back(partial)
    *partial, pool = ffn(second, stored + far, pool)
    early = settle(together(early, pool), planes)
    late = [partial[0]] + sent_on(together(partial[1:], early))
    home[0] = tie(home[0], early)
    early = exchange(early).reshape(planes * CAP, width)
    *partial, pool = ffn(home, stored + far, pool)
    early, *late = together([early] + late, pool)
    late = settle(late, planes)
    partial = together(partial, early, late)
    late = exchange(late).reshape(planes * CAP, width)
    home = added(*back(partial))
    pool = tie(pool, early)
    for axis in ("z", "t", "d"):
        size = lax.axis_size({"t": "tensor", "z": "expert", "d": "dp"}[axis])
        pool = sum([swap(pool, **{axis: step}) for step in range(1, size)], pool)
    parts = (early, home[:CAP], swap(late, t=1), swap(home[CAP:], t=1))
    embedded = combine(tokens, weights, parts)

    pooled = pool[:, :width] / pool[:, width : width + 1]
    return (embedded, pooled)


def slot_numbers(routes):
    flat_routes = routes.reshape(-1)
    pairs = flat_routes.shape[0]
    same = flat_routes[:, None] == flat_routes[None, :]
    earlier = jnp.arange(pairs)[None, :] < jnp.arange(pairs)[:, None]
    slot_rank = jnp.sum((same & earlier).astype(jnp.int32), axis=1)
    return flat_routes * CAP + slot_rank


def shards(tokens, routes, gates, segments, w_gate, w_up, w_down):
    tok_count, width = tokens.shape
    experts_axis = lax.axis_size("expert")
    per_device = w_gate.shape[0]
    replicas = max(1, experts_axis // EXPERTS)
    plane = lax.axis_size("dp") * lax.axis_size("tensor")
    values = tokens.astype(jnp.float32)
    scale = lax.rsqrt(jnp.mean(values * values, axis=1, keepdims=True) + epsilon)
    normed = (values * scale).astype(jnp.bfloat16)
    slot_index = slot_numbers(routes)
    hits = jnp.arange(EXPERTS * CAP, dtype=jnp.int32)[:, None] == slot_index[None, :]
    placing = jnp.sum(hits.astype(jnp.int32).reshape(EXPERTS * CAP, tok_count, TOP), axis=2)
    slot_rows = jnp.dot(placing.astype(jnp.bfloat16), normed, preferred_element_type=jnp.float32)
    shaped = slot_rows.astype(jnp.bfloat16).reshape(EXPERTS, CAP, width)
    if replicas > 1:
        shaped = jnp.repeat(shaped, replicas, axis=0)
    send_rows = shaped.reshape(EXPERTS * replicas * CAP, width)
    received = lax.all_to_all(send_rows, "expert", split_axis=0, concat_axis=0, tiled=True)
    local_rows = received.reshape(experts_axis, per_device, CAP, width)
    block = lax.all_gather(local_rows, ("dp", "tensor"), axis=0, tiled=True)
    gate_proj = jnp.einsum("nacd,adf->nacf", block, w_gate, preferred_element_type=jnp.float32)
    up_proj = jnp.einsum("nacd,adf->nacf", block, w_up, preferred_element_type=jnp.float32)
    hidden = (jax.nn.silu(gate_proj) * up_proj).astype(jnp.bfloat16)
    summed = lax.psum_scatter(
        jnp.einsum("nacf,afd->nacd", hidden, w_down, preferred_element_type=jnp.float32).astype(jnp.bfloat16),
        ("dp", "tensor"),
        scatter_dimension=0,
        tiled=True,
    )
    returned = lax.all_to_all(summed, "expert", split_axis=0, concat_axis=0, tiled=True).astype(jnp.float32)
    expert_out = jnp.sum(returned.reshape(EXPERTS, replicas, CAP, width), axis=1)
    picked = jnp.take(expert_out.reshape(EXPERTS * CAP, width), slot_index, axis=0).reshape(tok_count, TOP, width)
    embedded = (values + jnp.sum(gates[:, :, None] * picked, axis=1)).astype(jnp.bfloat16)
    seq_total = tok_count * plane * experts_axis // 256
    seq_hot = jnp.arange(seq_total, dtype=jnp.int32)[:, None] == segments[None, :]
    seq_sums = jnp.dot(seq_hot.astype(jnp.bfloat16), embedded, preferred_element_type=jnp.float32)
    seq_counts = jnp.sum(seq_hot.astype(jnp.float32), axis=1)
    total_sums, total_counts = lax.psum((seq_sums, seq_counts), AXES)
    return (embedded, total_sums / total_counts[:, None])


def solution(mesh):
    placed = (
        P(AXES, None),
        P(AXES, None),
        P(AXES, None),
        P(AXES),
        P("expert", None, ("dp", "tensor")),
        P("expert", None, ("dp", "tensor")),
        P("expert", ("dp", "tensor"), None),
    )
    dp, tensor, planes = (mesh.shape[name] for name in AXES)
    paired = dp == 4 and tensor == 2 and EXPERTS == tensor * planes and xor_steps(planes)
    return jax.shard_map(
        core_shards if paired else shards,
        mesh=mesh,
        in_specs=placed,
        out_specs=(P(AXES, None), P()),
        check_vma=False,
    )
```

```python
import functools

import jax
import jax.numpy as jnp
from jax import lax
from jax.experimental import pallas as pl
from jax.experimental.pallas import tpu as pltpu
from jax.sharding import PartitionSpec as P

EXPERTS = 8
TOP = 2
CAP = 24
LANES = 128
VMEM_LIMIT = 48 << 20
AXES = ("dp", "tensor", "expert")


epsilon = 1e-06


def xor_steps(size):
    return size & (size - 1) == 0


def swap(x, d=0, t=0, z=0, turned=None):
    sizes = [lax.axis_size(name) for name in AXES]
    pairs = []
    for i in range(sizes[0]):
        for j in range(sizes[1]):
            for k in range(sizes[2]):
                flip = d if turned is None or j % 2 == 0 else turned
                here = (i * sizes[1] + j) * sizes[2] + k
                there = ((i ^ flip) * sizes[1] + (j ^ t)) * sizes[2] + (k ^ z)
                pairs.append((here, there))
    return lax.ppermute(x, AXES, pairs)


def prep_kernel(seqs, planes, tokens, routes, gates, seg_row, own, own_home, other, other_home, weights, sums):
    tok_count, width = tokens.shape
    slots = 2 * (planes + 1) * CAP
    t, z = lax.axis_index("tensor"), lax.axis_index("expert")
    raw = tokens[...]
    values = raw.astype(jnp.float32)
    scale = lax.rsqrt(jnp.mean(values * values, axis=1, keepdims=True) + epsilon)
    normed = (values * scale).astype(jnp.bfloat16)

    expert = lax.broadcasted_iota(jnp.int32, (EXPERTS, tok_count), 0)
    hot = [expert == routes[k : k + 1, :] for k in range(TOP)]
    named = (hot[0] | hot[1]).astype(jnp.bfloat16)
    earlier = (
        lax.broadcasted_iota(jnp.int32, (tok_count, tok_count), 0)
        < lax.broadcasted_iota(jnp.int32, (tok_count, tok_count), 1)
    ).astype(jnp.bfloat16)
    before = jnp.dot(named, earlier, preferred_element_type=jnp.float32)

    row = lax.broadcasted_iota(jnp.int32, (slots, tok_count), 0)
    group = row // CAP
    rank = row - group * CAP
    side = group // (planes + 1)
    plane = group - side * (planes + 1)
    row_expert = 2 * jnp.where(plane == planes, z, jnp.where(plane == z, EXPERTS, plane)) + (t ^ side)
    place = jnp.zeros((slots, tok_count), jnp.float32)
    weight = jnp.zeros((slots, tok_count), jnp.float32)
    for k in range(TOP):
        own_rank = jnp.sum(jnp.where(hot[k], before, 0.0), axis=0, keepdims=True).astype(jnp.int32)
        hit = (row_expert == routes[k : k + 1, :]) & (rank == own_rank)
        place = place + jnp.where(hit, 1.0, 0.0)
        weight = weight + jnp.where(hit, gates[k : k + 1, :], 0.0)
    weights[...] = weight

    rows = jnp.dot(place.astype(jnp.bfloat16), normed, preferred_element_type=jnp.float32).astype(jnp.bfloat16)
    high = weight.astype(jnp.bfloat16)
    low = (weight - high.astype(jnp.float32)).astype(jnp.bfloat16)
    lane = lax.broadcasted_iota(jnp.int32, (LANES, tok_count), 0)
    nt = (((1,), (1,)), ((), ()))
    marks = jnp.zeros((slots, LANES), jnp.float32)
    for part, first in ((high, 0), (low, seqs)):
        member = (lane == seg_row[...] + first).astype(jnp.bfloat16)
        marks = marks + lax.dot_general(part, member, nt, preferred_element_type=jnp.float32)
    marks = marks.astype(jnp.bfloat16)
    start = 0
    for out in (own, own_home, other, other_home):
        stop = start + out.shape[0]
        out[:, :width] = rows[start:stop]
        out[:, width:] = marks[start:stop]
        start = stop

    seq_hot = lax.broadcasted_iota(jnp.int32, (seqs, tok_count), 0) == seg_row[...]
    sums[:, :width] = jnp.dot(seq_hot.astype(jnp.bfloat16), raw, preferred_element_type=jnp.float32)
    counts = jnp.sum(seq_hot.astype(jnp.float32), axis=1, keepdims=True)
    sums[:, width:] = jnp.broadcast_to(counts, (seqs, LANES))


def prep(tokens, routes, gates, segments, seqs, planes):
    tok_count, width = tokens.shape
    vmem = pl.BlockSpec(memory_space=pltpu.VMEM)
    blocks = [
        jax.ShapeDtypeStruct((count * CAP, width + LANES), jnp.bfloat16) for count in (planes, 1, planes, 1)
    ]
    return pl.pallas_call(
        functools.partial(prep_kernel, seqs, planes),
        out_shape=(
            *blocks,
            jax.ShapeDtypeStruct((2 * (planes + 1) * CAP, tok_count), jnp.float32),
            jax.ShapeDtypeStruct((seqs, width + LANES), jnp.float32),
        ),
        in_specs=[vmem] * 4,
        out_specs=(vmem,) * 6,
        name="prep",
    )(tokens, routes.T, gates.T, segments[None, :])


def spans_of(total, tile):
    return [(start, min(tile, total - start)) for start in range(0, total, tile)]


def tie(value, *before):
    return lax.optimization_barrier((value,) + before)[0]


def ffn_kernel(pieces, tile, cols, depth, seqs, pool_in, *refs):
    parts, weights, outs = refs[:pieces], refs[pieces : pieces + 6], refs[pieces + 6 : 2 * pieces + 6]
    pool_out, rows_buf, gate_buf, up_buf, down_buf, hidden, row_sem, in_sem, down_sem = refs[2 * pieces + 6 :]
    t = lax.axis_index("tensor")
    halves = [[w.at[t] for w in weights[:3]], [w.at[t] for w in weights[3:]]]
    size = parts[0].shape[0]
    _, units, width = weights[0].shape
    row_copies = [
        pltpu.make_async_copy(parts[i], rows_buf.at[i, pl.ds(0, size)], row_sem.at[i]) for i in range(pieces)
    ]
    padded = rows_buf.shape[1]
    if padded > size:
        for i in range(pieces):
            rows_buf[i, size:] = jnp.zeros((padded - size, rows_buf.shape[2]), rows_buf.dtype)
    spans = spans_of(units, tile)
    col_spans = spans_of(width, cols)
    copies = []
    for h in range(2):
        for j, (start, length) in enumerate(spans):
            here = pl.ds(start, length)
            copies.append(
                [
                    pltpu.make_async_copy(halves[h][m].at[here], buf.at[h, here], in_sem.at[m, h * len(spans) + j])
                    for m, buf in enumerate((gate_buf, up_buf))
                ]
            )
    for j, (start, length) in enumerate(col_spans):
        here = pl.ds(start, length)
        copies.append(
            [
                pltpu.make_async_copy(
                    halves[h][2].at[:, here], down_buf.at[pl.ds(h * units, units), here], down_sem.at[h, j]
                )
                for h in range(2)
            ]
        )
    for copy in row_copies:
        copy.start()
    for group in copies[:depth]:
        for copy in group:
            copy.start()

    def arrive(i):
        for copy in copies[i]:
            copy.wait()
        for group in copies[i + depth : i + depth + 1]:
            for copy in group:
                copy.start()

    for copy in row_copies:
        copy.wait()
    x = rows_buf[:, :, :width].reshape(pieces * padded, width)
    marks = rows_buf[:, :, width:].reshape(pieces * padded, LANES).astype(jnp.float32).T[: 2 * seqs].astype(jnp.bfloat16)
    nt = (((1,), (1,)), ((), ()))
    for h in range(2):
        for j, (start, length) in enumerate(spans):
            arrive(h * len(spans) + j)
            here = slice(start, start + length)
            g = lax.dot_general(x, gate_buf[h, here], nt, preferred_element_type=jnp.float32)
            u = lax.dot_general(x, up_buf[h, here], nt, preferred_element_type=jnp.float32)
            value = g / (1.0 + jnp.exp(-g)) * u
            hidden[:, h * units + start : h * units + start + length] = value.astype(jnp.bfloat16)
    pool_out[:, width:] = pool_in[:, width:]
    for j, (start, length) in enumerate(col_spans):
        arrive(2 * len(spans) + j)
        here = slice(start, start + length)
        y = jnp.dot(hidden[...], down_buf[:, here], preferred_element_type=jnp.float32).astype(jnp.bfloat16)
        share = jnp.dot(marks, y, preferred_element_type=jnp.float32)
        pool_out[:, here] = pool_in[:, here] + share[:seqs] + share[seqs:]
        for i in range(pieces):
            outs[i][:, here] = y[i * padded : i * padded + size]


def ffn(parts, weights, pool):
    pieces = len(parts)
    size = parts[0].shape[0]
    _, units, width = weights[0].shape
    tile, cols, depth = 256, 768, 3
    padded = -(-size // 16) * 16
    rows = pieces * padded
    anywhere = pl.BlockSpec(memory_space=pl.ANY)
    vmem = pl.BlockSpec(memory_space=pltpu.VMEM)
    return pl.pallas_call(
        functools.partial(ffn_kernel, pieces, tile, cols, depth, pool.shape[0]),
        out_shape=(jax.ShapeDtypeStruct((size, width), jnp.bfloat16),) * pieces
        + (jax.ShapeDtypeStruct(pool.shape, pool.dtype),),
        in_specs=[vmem] + [anywhere] * (pieces + 6),
        out_specs=(vmem,) * (pieces + 1),
        scratch_shapes=[
            pltpu.VMEM((pieces, padded, width + LANES), jnp.bfloat16),
            pltpu.VMEM((2, units, width), jnp.bfloat16),
            pltpu.VMEM((2, units, width), jnp.bfloat16),
            pltpu.VMEM((2 * units, width), jnp.bfloat16),
            pltpu.VMEM((rows, 2 * units), jnp.bfloat16),
            pltpu.SemaphoreType.DMA((pieces,)),
            pltpu.SemaphoreType.DMA((2, 2 * len(spans_of(units, tile)))),
            pltpu.SemaphoreType.DMA((2, len(spans_of(width, cols)))),
        ],
        compiler_params=pltpu.CompilerParams(vmem_limit_bytes=VMEM_LIMIT),
        cost_estimate=pl.CostEstimate(
            flops=12 * rows * width * units, transcendentals=2 * rows * units, bytes_accessed=12 * units * width
        ),
        name="ffn",
    )(pool, *parts, *weights)


def settle_kernel(planes, *refs):
    parts, out = refs[:-1], refs[-1]
    z = lax.axis_index("expert")
    total = parts[0][...].astype(jnp.float32)
    for part in parts[1:]:
        total = total + part[...].astype(jnp.float32)
    for j in range(planes - 1):
        out[lax.rem(z + 1 + j, planes)] = total[j * CAP : (j + 1) * CAP].astype(jnp.bfloat16)
    out[z] = jnp.zeros(out.shape[1:], jnp.bfloat16)


def settle(parts, planes):
    vmem = pl.BlockSpec(memory_space=pltpu.VMEM)
    return pl.pallas_call(
        functools.partial(settle_kernel, planes),
        out_shape=jax.ShapeDtypeStruct((planes, CAP, parts[0].shape[1]), jnp.bfloat16),
        in_specs=[vmem] * len(parts),
        out_specs=vmem,
        name="settle",
    )(*parts)


def combine_kernel(planes, tokens, weights, early, home, sibling_home, *refs):
    late, out = refs[:-1], refs[-1]
    z = lax.axis_index("expert")
    mixed = jnp.zeros(tokens.shape, jnp.float32)
    half = (planes + 1) * CAP
    parts = [(early, 0), (home, planes * CAP), (sibling_home, half + planes * CAP)]
    for j, part in enumerate(late):
        plane = lax.rem(z + planes - 1 - j, planes)
        parts.append((part, pl.multiple_of(half + plane * CAP, 8)))
    for part, start in parts:
        weight = weights[pl.ds(start, part.shape[0])].T
        high = weight.astype(jnp.bfloat16)
        low = (weight - high.astype(jnp.float32)).astype(jnp.bfloat16)
        for factor in (low, high):
            mixed = mixed + jnp.dot(factor, part[...], preferred_element_type=jnp.float32)
    out[...] = (tokens[...].astype(jnp.float32) + mixed).astype(jnp.bfloat16)


def combine(tokens, weights, early, home, sibling_home, late):
    vmem = pl.BlockSpec(memory_space=pltpu.VMEM)
    return pl.pallas_call(
        functools.partial(combine_kernel, len(late) + 1),
        out_shape=jax.ShapeDtypeStruct(tokens.shape, jnp.bfloat16),
        in_specs=[vmem] * (5 + len(late)),
        out_specs=vmem,
        name="combine",
    )(tokens, weights, early, home, sibling_home, *late)


def added(*arrays):
    total = arrays[0].astype(jnp.float32)
    for array in arrays[1:]:
        total = total + array.astype(jnp.float32)
    return total.astype(jnp.bfloat16)


def core_shards(tokens, routes, gates, segments, w_gate, w_up, w_down):
    tok_count, width = tokens.shape
    chips, cores, planes = (lax.axis_size(name) for name in AXES)
    seqs = tok_count * chips * cores * planes // 256

    own, own_home, other, other_home, weights, pool = prep(tokens, routes, gates, segments, seqs, planes)
    sibling, sibling_home = swap(other, t=1), swap(other_home, t=1)
    stored = (jnp.swapaxes(w_gate, 1, 2), jnp.swapaxes(w_up, 1, 2), w_down)

    tied = lax.optimization_barrier(stored + (sibling, sibling_home))
    far = tuple(pltpu.with_memory_space_constraint(swap(array, t=1), pltpu.HBM) for array in tied[:3])

    z = lax.axis_index("expert")
    others = (planes - 1) * CAP

    def exchange(rows):
        return lax.all_to_all(rows, "expert", split_axis=0, concat_axis=0, tiled=True)

    def turn(block, step):
        return lax.ppermute(block, "expert", [(i, (i + step) % planes) for i in range(planes)])

    def outward(rows):
        return lax.dynamic_slice_in_dim(jnp.concatenate([rows, rows]), (z + 1) * CAP, others)

    def sent_on(arrays):
        return [swap(array, d=step, turned=turned) for array, (step, turned) in zip(arrays, ((1, 2), (2, 1), (3, 3)))]

    def together(arrays, *before):
        return list(lax.optimization_barrier(tuple(arrays) + before))[: len(arrays)]

    home = jnp.concatenate([own_home, sibling_home])
    arrived = exchange(own)
    home_near, home_side = swap(home, d=1, turned=2), swap(home, d=2, turned=1)
    arrived, home_near = together([arrived], home_near)[0], home_near
    early = outward(arrived)
    near, side = swap(early, d=1, turned=2), swap(early, d=2, turned=1)
    late = outward(exchange(tie(sibling, early)))
    first = [early, near, side, swap(near, d=2, turned=1)]
    home = [home, home_near, home_side, swap(home_near, d=2, turned=1)]
    second = [late] + sent_on([late] * 3)

    def back(parts):
        return [parts[0]] + sent_on(parts[1:])

    *partial, pool = ffn(first, stored + far, pool)
    early = back(partial)
    *partial, pool = ffn(second, stored + far, pool)
    early = settle(together(early, pool), planes)
    late = [partial[0]] + sent_on(together(partial[1:], early))
    home[0] = tie(home[0], early)
    early = exchange(early).reshape(planes * CAP, width)
    *partial, pool = ffn(home, stored + far, pool)
    early, *late = together([early] + late, pool)
    late = added(*late)
    partial = together(partial, early, late)
    home = added(*back(partial))
    late = [turn(late[(j - 1) * CAP : j * CAP], j) for j in range(1, planes)]
    pool = tie(pool, early)
    for axis in ("z", "t", "d"):
        size = lax.axis_size({"t": "tensor", "z": "expert", "d": "dp"}[axis])
        pool = sum([swap(pool, **{axis: step}) for step in range(1, size)], pool)
    late = [swap(block, t=1) for block in late]
    embedded = combine(tokens, weights, early, home[:CAP], swap(home[CAP:], t=1), late)

    pooled = pool[:, :width] / pool[:, width : width + 1]
    return (embedded, pooled)


def slot_numbers(routes):
    flat_routes = routes.reshape(-1)
    pairs = flat_routes.shape[0]
    same = flat_routes[:, None] == flat_routes[None, :]
    earlier = jnp.arange(pairs)[None, :] < jnp.arange(pairs)[:, None]
    slot_rank = jnp.sum((same & earlier).astype(jnp.int32), axis=1)
    return flat_routes * CAP + slot_rank


def shards(tokens, routes, gates, segments, w_gate, w_up, w_down):
    tok_count, width = tokens.shape
    experts_axis = lax.axis_size("expert")
    per_device = w_gate.shape[0]
    replicas = max(1, experts_axis // EXPERTS)
    plane = lax.axis_size("dp") * lax.axis_size("tensor")
    values = tokens.astype(jnp.float32)
    scale = lax.rsqrt(jnp.mean(values * values, axis=1, keepdims=True) + epsilon)
    normed = (values * scale).astype(jnp.bfloat16)
    slot_index = slot_numbers(routes)
    hits = jnp.arange(EXPERTS * CAP, dtype=jnp.int32)[:, None] == slot_index[None, :]
    placing = jnp.sum(hits.astype(jnp.int32).reshape(EXPERTS * CAP, tok_count, TOP), axis=2)
    slot_rows = jnp.dot(placing.astype(jnp.bfloat16), normed, preferred_element_type=jnp.float32)
    shaped = slot_rows.astype(jnp.bfloat16).reshape(EXPERTS, CAP, width)
    if replicas > 1:
        shaped = jnp.repeat(shaped, replicas, axis=0)
    send_rows = shaped.reshape(EXPERTS * replicas * CAP, width)
    received = lax.all_to_all(send_rows, "expert", split_axis=0, concat_axis=0, tiled=True)
    local_rows = received.reshape(experts_axis, per_device, CAP, width)
    block = lax.all_gather(local_rows, ("dp", "tensor"), axis=0, tiled=True)
    gate_proj = jnp.einsum("nacd,adf->nacf", block, w_gate, preferred_element_type=jnp.float32)
    up_proj = jnp.einsum("nacd,adf->nacf", block, w_up, preferred_element_type=jnp.float32)
    hidden = (jax.nn.silu(gate_proj) * up_proj).astype(jnp.bfloat16)
    summed = lax.psum_scatter(
        jnp.einsum("nacf,afd->nacd", hidden, w_down, preferred_element_type=jnp.float32).astype(jnp.bfloat16),
        ("dp", "tensor"),
        scatter_dimension=0,
        tiled=True,
    )
    returned = lax.all_to_all(summed, "expert", split_axis=0, concat_axis=0, tiled=True).astype(jnp.float32)
    expert_out = jnp.sum(returned.reshape(EXPERTS, replicas, CAP, width), axis=1)
    picked = jnp.take(expert_out.reshape(EXPERTS * CAP, width), slot_index, axis=0).reshape(tok_count, TOP, width)
    embedded = (values + jnp.sum(gates[:, :, None] * picked, axis=1)).astype(jnp.bfloat16)
    seq_total = tok_count * plane * experts_axis // 256
    seq_hot = jnp.arange(seq_total, dtype=jnp.int32)[:, None] == segments[None, :]
    seq_sums = jnp.dot(seq_hot.astype(jnp.bfloat16), embedded, preferred_element_type=jnp.float32)
    seq_counts = jnp.sum(seq_hot.astype(jnp.float32), axis=1)
    total_sums, total_counts = lax.psum((seq_sums, seq_counts), AXES)
    return (embedded, total_sums / total_counts[:, None])


def solution(mesh):
    placed = (
        P(AXES, None),
        P(AXES, None),
        P(AXES, None),
        P(AXES),
        P("expert", None, ("dp", "tensor")),
        P("expert", None, ("dp", "tensor")),
        P("expert", ("dp", "tensor"), None),
    )
    dp, tensor, planes = (mesh.shape[name] for name in AXES)
    paired = dp == 4 and tensor == 2 and EXPERTS == tensor * planes and xor_steps(planes)
    return jax.shard_map(
        core_shards if paired else shards,
        mesh=mesh,
        in_specs=placed,
        out_specs=(P(AXES, None), P()),
        check_vma=False,
    )
```

```python
import functools

import jax
import jax.numpy as jnp
from jax import lax
from jax.experimental import pallas as pl
from jax.experimental.pallas import tpu as pltpu
from jax.sharding import PartitionSpec as P

EXPERTS = 8
TOP = 2
CAP = 24
LANES = 128
VMEM_LIMIT = 48 << 20
AXES = ("dp", "tensor", "expert")


epsilon = 1e-06


def xor_steps(size):
    return size & (size - 1) == 0


def swap(x, d=0, t=0, z=0, turned=None):
    sizes = [lax.axis_size(name) for name in AXES]
    pairs = []
    for i in range(sizes[0]):
        for j in range(sizes[1]):
            for k in range(sizes[2]):
                flip = d if turned is None or j % 2 == 0 else turned
                here = (i * sizes[1] + j) * sizes[2] + k
                there = ((i ^ flip) * sizes[1] + (j ^ t)) * sizes[2] + (k ^ z)
                pairs.append((here, there))
    return lax.ppermute(x, AXES, pairs)


def prep_kernel(seqs, planes, tokens, routes, gates, seg_row, own, own_home, other, other_home, weights, sums):
    tok_count, width = tokens.shape
    slots = 2 * (planes + 1) * CAP
    t, z = lax.axis_index("tensor"), lax.axis_index("expert")
    raw = tokens[...]
    values = raw.astype(jnp.float32)
    scale = lax.rsqrt(jnp.mean(values * values, axis=1, keepdims=True) + epsilon)
    normed = (values * scale).astype(jnp.bfloat16)

    expert = lax.broadcasted_iota(jnp.int32, (EXPERTS, tok_count), 0)
    hot = [expert == routes[k : k + 1, :] for k in range(TOP)]
    named = (hot[0] | hot[1]).astype(jnp.bfloat16)
    earlier = (
        lax.broadcasted_iota(jnp.int32, (tok_count, tok_count), 0)
        < lax.broadcasted_iota(jnp.int32, (tok_count, tok_count), 1)
    ).astype(jnp.bfloat16)
    before = jnp.dot(named, earlier, preferred_element_type=jnp.float32)

    row = lax.broadcasted_iota(jnp.int32, (slots, tok_count), 0)
    group = row // CAP
    rank = row - group * CAP
    side = group // (planes + 1)
    plane = group - side * (planes + 1)
    row_expert = 2 * jnp.where(plane == planes, z, jnp.where(plane == z, EXPERTS, plane)) + (t ^ side)
    place = jnp.zeros((slots, tok_count), jnp.float32)
    weight = jnp.zeros((slots, tok_count), jnp.float32)
    for k in range(TOP):
        own_rank = jnp.sum(jnp.where(hot[k], before, 0.0), axis=0, keepdims=True).astype(jnp.int32)
        hit = (row_expert == routes[k : k + 1, :]) & (rank == own_rank)
        place = place + jnp.where(hit, 1.0, 0.0)
        weight = weight + jnp.where(hit, gates[k : k + 1, :], 0.0)
    weights[...] = weight

    rows = jnp.dot(place.astype(jnp.bfloat16), normed, preferred_element_type=jnp.float32).astype(jnp.bfloat16)
    high = weight.astype(jnp.bfloat16)
    low = (weight - high.astype(jnp.float32)).astype(jnp.bfloat16)
    lane = lax.broadcasted_iota(jnp.int32, (LANES, tok_count), 0)
    nt = (((1,), (1,)), ((), ()))
    marks = jnp.zeros((slots, LANES), jnp.float32)
    for part, first in ((high, 0), (low, seqs)):
        member = (lane == seg_row[...] + first).astype(jnp.bfloat16)
        marks = marks + lax.dot_general(part, member, nt, preferred_element_type=jnp.float32)
    marks = marks.astype(jnp.bfloat16)
    start = 0
    for out in (own, own_home, other, other_home):
        stop = start + out.shape[0]
        out[:, :width] = rows[start:stop]
        out[:, width:] = marks[start:stop]
        start = stop

    seq_hot = lax.broadcasted_iota(jnp.int32, (seqs, tok_count), 0) == seg_row[...]
    sums[:, :width] = jnp.dot(seq_hot.astype(jnp.bfloat16), raw, preferred_element_type=jnp.float32)
    counts = jnp.sum(seq_hot.astype(jnp.float32), axis=1, keepdims=True)
    sums[:, width:] = jnp.broadcast_to(counts, (seqs, LANES))


def prep(tokens, routes, gates, segments, seqs, planes):
    tok_count, width = tokens.shape
    vmem = pl.BlockSpec(memory_space=pltpu.VMEM)
    blocks = [
        jax.ShapeDtypeStruct((count * CAP, width + LANES), jnp.bfloat16) for count in (planes, 1, planes, 1)
    ]
    return pl.pallas_call(
        functools.partial(prep_kernel, seqs, planes),
        out_shape=(
            *blocks,
            jax.ShapeDtypeStruct((2 * (planes + 1) * CAP, tok_count), jnp.float32),
            jax.ShapeDtypeStruct((seqs, width + LANES), jnp.float32),
        ),
        in_specs=[vmem] * 4,
        out_specs=(vmem,) * 6,
        name="prep",
    )(tokens, routes.T, gates.T, segments[None, :])


def spans_of(total, tile):
    return [(start, min(tile, total - start)) for start in range(0, total, tile)]


def tie(value, *before):
    return lax.optimization_barrier((value,) + before)[0]


def ffn_kernel(pieces, tile, cols, depth, seqs, pool_in, *refs):
    parts, weights, outs = refs[:pieces], refs[pieces : pieces + 6], refs[pieces + 6 : 2 * pieces + 6]
    pool_out, rows_buf, gate_buf, up_buf, down_buf, hidden, row_sem, in_sem, down_sem = refs[2 * pieces + 6 :]
    t = lax.axis_index("tensor")
    halves = [[w.at[t] for w in weights[:3]], [w.at[t] for w in weights[3:]]]
    size = parts[0].shape[0]
    _, units, width = weights[0].shape
    row_copies = [
        pltpu.make_async_copy(parts[i], rows_buf.at[i, pl.ds(0, size)], row_sem.at[i]) for i in range(pieces)
    ]
    padded = rows_buf.shape[1]
    if padded > size:
        for i in range(pieces):
            rows_buf[i, size:] = jnp.zeros((padded - size, rows_buf.shape[2]), rows_buf.dtype)
    spans = spans_of(units, tile)
    col_spans = spans_of(width, cols)
    copies = []
    for h in range(2):
        for j, (start, length) in enumerate(spans):
            here = pl.ds(start, length)
            copies.append(
                [
                    pltpu.make_async_copy(halves[h][m].at[here], buf.at[h, here], in_sem.at[m, h * len(spans) + j])
                    for m, buf in enumerate((gate_buf, up_buf))
                ]
            )
    for j, (start, length) in enumerate(col_spans):
        here = pl.ds(start, length)
        copies.append(
            [
                pltpu.make_async_copy(
                    halves[h][2].at[:, here], down_buf.at[pl.ds(h * units, units), here], down_sem.at[h, j]
                )
                for h in range(2)
            ]
        )
    for group in copies[:1]:
        for copy in group:
            copy.start()
    for copy in row_copies:
        copy.start()
    for group in copies[1:depth]:
        for copy in group:
            copy.start()

    def arrive(i):
        for copy in copies[i]:
            copy.wait()
        for group in copies[i + depth : i + depth + 1]:
            for copy in group:
                copy.start()

    for copy in row_copies:
        copy.wait()
    x = rows_buf[:, :, :width].reshape(pieces * padded, width)
    marks = rows_buf[:, :, width:].reshape(pieces * padded, LANES).astype(jnp.float32).T[: 2 * seqs].astype(jnp.bfloat16)
    nt = (((1,), (1,)), ((), ()))
    for h in range(2):
        for j, (start, length) in enumerate(spans):
            arrive(h * len(spans) + j)
            here = slice(start, start + length)
            g = lax.dot_general(x, gate_buf[h, here], nt, preferred_element_type=jnp.float32)
            u = lax.dot_general(x, up_buf[h, here], nt, preferred_element_type=jnp.float32)
            value = g / (1.0 + jnp.exp(-g)) * u
            hidden[:, h * units + start : h * units + start + length] = value.astype(jnp.bfloat16)
    pool_out[:, width:] = pool_in[:, width:]
    for j, (start, length) in enumerate(col_spans):
        arrive(2 * len(spans) + j)
        here = slice(start, start + length)
        y = jnp.dot(hidden[...], down_buf[:, here], preferred_element_type=jnp.float32).astype(jnp.bfloat16)
        share = jnp.dot(marks, y, preferred_element_type=jnp.float32)
        pool_out[:, here] = pool_in[:, here] + share[:seqs] + share[seqs:]
        for i in range(pieces):
            outs[i][:, here] = y[i * padded : i * padded + size]


def ffn(parts, weights, pool):
    pieces = len(parts)
    size = parts[0].shape[0]
    _, units, width = weights[0].shape
    tile, cols, depth = 256, 768, 4
    padded = -(-size // 16) * 16
    rows = pieces * padded
    anywhere = pl.BlockSpec(memory_space=pl.ANY)
    vmem = pl.BlockSpec(memory_space=pltpu.VMEM)
    return pl.pallas_call(
        functools.partial(ffn_kernel, pieces, tile, cols, depth, pool.shape[0]),
        out_shape=(jax.ShapeDtypeStruct((size, width), jnp.bfloat16),) * pieces
        + (jax.ShapeDtypeStruct(pool.shape, pool.dtype),),
        in_specs=[vmem] + [anywhere] * (pieces + 6),
        out_specs=(vmem,) * (pieces + 1),
        scratch_shapes=[
            pltpu.VMEM((pieces, padded, width + LANES), jnp.bfloat16),
            pltpu.VMEM((2, units, width), jnp.bfloat16),
            pltpu.VMEM((2, units, width), jnp.bfloat16),
            pltpu.VMEM((2 * units, width), jnp.bfloat16),
            pltpu.VMEM((rows, 2 * units), jnp.bfloat16),
            pltpu.SemaphoreType.DMA((pieces,)),
            pltpu.SemaphoreType.DMA((2, 2 * len(spans_of(units, tile)))),
            pltpu.SemaphoreType.DMA((2, len(spans_of(width, cols)))),
        ],
        compiler_params=pltpu.CompilerParams(vmem_limit_bytes=VMEM_LIMIT),
        cost_estimate=pl.CostEstimate(
            flops=12 * rows * width * units, transcendentals=2 * rows * units, bytes_accessed=12 * units * width
        ),
        name="ffn",
    )(pool, *parts, *weights)


def settle_kernel(planes, *refs):
    parts, out = refs[:-1], refs[-1]
    z = lax.axis_index("expert")
    total = parts[0][...].astype(jnp.float32)
    for part in parts[1:]:
        total = total + part[...].astype(jnp.float32)
    for j in range(planes - 1):
        out[lax.rem(z + 1 + j, planes)] = total[j * CAP : (j + 1) * CAP].astype(jnp.bfloat16)
    out[z] = jnp.zeros(out.shape[1:], jnp.bfloat16)


def settle(parts, planes):
    vmem = pl.BlockSpec(memory_space=pltpu.VMEM)
    return pl.pallas_call(
        functools.partial(settle_kernel, planes),
        out_shape=jax.ShapeDtypeStruct((planes, CAP, parts[0].shape[1]), jnp.bfloat16),
        in_specs=[vmem] * len(parts),
        out_specs=vmem,
        name="settle",
    )(*parts)


def combine_kernel(planes, tokens, weights, early, home, sibling_home, *refs):
    late, out = refs[:-1], refs[-1]
    z = lax.axis_index("expert")
    mixed = jnp.zeros(tokens.shape, jnp.float32)
    half = (planes + 1) * CAP
    parts = [(early, 0), (home, planes * CAP), (sibling_home, half + planes * CAP)]
    for j, part in enumerate(late):
        plane = lax.rem(z + planes - 1 - j, planes)
        parts.append((part, pl.multiple_of(half + plane * CAP, 8)))
    for part, start in parts:
        weight = weights[pl.ds(start, part.shape[0])].T
        high = weight.astype(jnp.bfloat16)
        low = (weight - high.astype(jnp.float32)).astype(jnp.bfloat16)
        for factor in (low, high):
            mixed = mixed + jnp.dot(factor, part[...], preferred_element_type=jnp.float32)
    out[...] = (tokens[...].astype(jnp.float32) + mixed).astype(jnp.bfloat16)


def combine(tokens, weights, early, home, sibling_home, late):
    vmem = pl.BlockSpec(memory_space=pltpu.VMEM)
    return pl.pallas_call(
        functools.partial(combine_kernel, len(late) + 1),
        out_shape=jax.ShapeDtypeStruct(tokens.shape, jnp.bfloat16),
        in_specs=[vmem] * (5 + len(late)),
        out_specs=vmem,
        name="combine",
    )(tokens, weights, early, home, sibling_home, *late)


def added(*arrays):
    total = arrays[0].astype(jnp.float32)
    for array in arrays[1:]:
        total = total + array.astype(jnp.float32)
    return total.astype(jnp.bfloat16)


def core_shards(tokens, routes, gates, segments, w_gate, w_up, w_down):
    tok_count, width = tokens.shape
    chips, cores, planes = (lax.axis_size(name) for name in AXES)
    seqs = tok_count * chips * cores * planes // 256

    own, own_home, other, other_home, weights, pool = prep(tokens, routes, gates, segments, seqs, planes)
    sibling, sibling_home = swap(other, t=1), swap(other_home, t=1)
    stored = (jnp.swapaxes(w_gate, 1, 2), jnp.swapaxes(w_up, 1, 2), w_down)

    tied = lax.optimization_barrier(stored + (sibling, sibling_home))
    far = tuple(pltpu.with_memory_space_constraint(swap(array, t=1), pltpu.HBM) for array in tied[:3])

    z = lax.axis_index("expert")
    others = (planes - 1) * CAP

    def exchange(rows):
        return lax.all_to_all(rows, "expert", split_axis=0, concat_axis=0, tiled=True)

    def turn(block, step):
        return lax.ppermute(block, "expert", [(i, (i + step) % planes) for i in range(planes)])

    def outward(rows):
        return lax.dynamic_slice_in_dim(jnp.concatenate([rows, rows]), (z + 1) * CAP, others)

    def sent_on(arrays):
        return [swap(array, d=step, turned=turned) for array, (step, turned) in zip(arrays, ((1, 2), (2, 1), (3, 3)))]

    def together(arrays, *before):
        return list(lax.optimization_barrier(tuple(arrays) + before))[: len(arrays)]

    home = jnp.concatenate([own_home, sibling_home])
    arrived = exchange(own)
    home_near, home_side = swap(home, d=1, turned=2), swap(home, d=2, turned=1)
    arrived, home_near = together([arrived], home_near)[0], home_near
    early = outward(arrived)
    near, side = swap(early, d=1, turned=2), swap(early, d=2, turned=1)
    late = outward(exchange(tie(sibling, early)))
    first = [early, near, side, swap(near, d=2, turned=1)]
    home = [home, home_near, home_side, swap(home_near, d=2, turned=1)]
    second = [late] + sent_on([late] * 3)

    def back(parts):
        return [parts[0]] + sent_on(parts[1:])

    *partial, pool = ffn(first, stored + far, pool)
    early = back(partial)
    *partial, pool = ffn(second, stored + far, pool)
    early = settle(together(early, pool), planes)
    late = [partial[0]] + sent_on(together(partial[1:], early))
    home[0] = tie(home[0], early)
    early = exchange(early).reshape(planes * CAP, width)
    *partial, pool = ffn(home, stored + far, pool)
    early, *late = together([early] + late, pool)
    late = added(*late)
    partial = together(partial, early)
    home = added(*back(partial))
    late = [turn(late[(j - 1) * CAP : j * CAP], j) for j in range(1, planes)]
    pool = tie(pool, early)
    for axis in ("z", "t", "d"):
        size = lax.axis_size({"t": "tensor", "z": "expert", "d": "dp"}[axis])
        pool = sum([swap(pool, **{axis: step}) for step in range(1, size)], pool)
    late = [swap(block, t=1) for block in late]
    embedded = combine(tokens, weights, early, home[:CAP], swap(home[CAP:], t=1), late)

    pooled = pool[:, :width] / pool[:, width : width + 1]
    return (embedded, pooled)


def slot_numbers(routes):
    flat_routes = routes.reshape(-1)
    pairs = flat_routes.shape[0]
    same = flat_routes[:, None] == flat_routes[None, :]
    earlier = jnp.arange(pairs)[None, :] < jnp.arange(pairs)[:, None]
    slot_rank = jnp.sum((same & earlier).astype(jnp.int32), axis=1)
    return flat_routes * CAP + slot_rank


def shards(tokens, routes, gates, segments, w_gate, w_up, w_down):
    tok_count, width = tokens.shape
    experts_axis = lax.axis_size("expert")
    per_device = w_gate.shape[0]
    replicas = max(1, experts_axis // EXPERTS)
    plane = lax.axis_size("dp") * lax.axis_size("tensor")
    values = tokens.astype(jnp.float32)
    scale = lax.rsqrt(jnp.mean(values * values, axis=1, keepdims=True) + epsilon)
    normed = (values * scale).astype(jnp.bfloat16)
    slot_index = slot_numbers(routes)
    hits = jnp.arange(EXPERTS * CAP, dtype=jnp.int32)[:, None] == slot_index[None, :]
    placing = jnp.sum(hits.astype(jnp.int32).reshape(EXPERTS * CAP, tok_count, TOP), axis=2)
    slot_rows = jnp.dot(placing.astype(jnp.bfloat16), normed, preferred_element_type=jnp.float32)
    shaped = slot_rows.astype(jnp.bfloat16).reshape(EXPERTS, CAP, width)
    if replicas > 1:
        shaped = jnp.repeat(shaped, replicas, axis=0)
    send_rows = shaped.reshape(EXPERTS * replicas * CAP, width)
    received = lax.all_to_all(send_rows, "expert", split_axis=0, concat_axis=0, tiled=True)
    local_rows = received.reshape(experts_axis, per_device, CAP, width)
    block = lax.all_gather(local_rows, ("dp", "tensor"), axis=0, tiled=True)
    gate_proj = jnp.einsum("nacd,adf->nacf", block, w_gate, preferred_element_type=jnp.float32)
    up_proj = jnp.einsum("nacd,adf->nacf", block, w_up, preferred_element_type=jnp.float32)
    hidden = (jax.nn.silu(gate_proj) * up_proj).astype(jnp.bfloat16)
    summed = lax.psum_scatter(
        jnp.einsum("nacf,afd->nacd", hidden, w_down, preferred_element_type=jnp.float32).astype(jnp.bfloat16),
        ("dp", "tensor"),
        scatter_dimension=0,
        tiled=True,
    )
    returned = lax.all_to_all(summed, "expert", split_axis=0, concat_axis=0, tiled=True).astype(jnp.float32)
    expert_out = jnp.sum(returned.reshape(EXPERTS, replicas, CAP, width), axis=1)
    picked = jnp.take(expert_out.reshape(EXPERTS * CAP, width), slot_index, axis=0).reshape(tok_count, TOP, width)
    embedded = (values + jnp.sum(gates[:, :, None] * picked, axis=1)).astype(jnp.bfloat16)
    seq_total = tok_count * plane * experts_axis // 256
    seq_hot = jnp.arange(seq_total, dtype=jnp.int32)[:, None] == segments[None, :]
    seq_sums = jnp.dot(seq_hot.astype(jnp.bfloat16), embedded, preferred_element_type=jnp.float32)
    seq_counts = jnp.sum(seq_hot.astype(jnp.float32), axis=1)
    total_sums, total_counts = lax.psum((seq_sums, seq_counts), AXES)
    return (embedded, total_sums / total_counts[:, None])


def solution(mesh):
    placed = (
        P(AXES, None),
        P(AXES, None),
        P(AXES, None),
        P(AXES),
        P("expert", None, ("dp", "tensor")),
        P("expert", None, ("dp", "tensor")),
        P("expert", ("dp", "tensor"), None),
    )
    dp, tensor, planes = (mesh.shape[name] for name in AXES)
    paired = dp == 4 and tensor == 2 and EXPERTS == tensor * planes and xor_steps(planes)
    return jax.shard_map(
        core_shards if paired else shards,
        mesh=mesh,
        in_specs=placed,
        out_specs=(P(AXES, None), P()),
        check_vma=False,
    )
```

```python
import functools

import jax
import jax.numpy as jnp
from jax import lax
from jax.experimental import pallas as pl
from jax.experimental.pallas import tpu as pltpu
from jax.sharding import PartitionSpec as P

EXPERTS = 8
TOP = 2
CAP = 24
LANES = 128
VMEM_LIMIT = 50 << 20
AXES = ("dp", "tensor", "expert")


epsilon = 1e-06


def xor_steps(size):
    return size & (size - 1) == 0


def swap(x, d=0, t=0, z=0, turned=None):
    sizes = [lax.axis_size(name) for name in AXES]
    pairs = []
    for i in range(sizes[0]):
        for j in range(sizes[1]):
            for k in range(sizes[2]):
                flip = d if turned is None or j % 2 == 0 else turned
                here = (i * sizes[1] + j) * sizes[2] + k
                there = ((i ^ flip) * sizes[1] + (j ^ t)) * sizes[2] + (k ^ z)
                pairs.append((here, there))
    return lax.ppermute(x, AXES, pairs)


def prep_kernel(seqs, planes, tokens, routes, gates, seg_row, own, own_home, other, other_home, weights, sums):
    tok_count, width = tokens.shape
    slots = 2 * (planes + 1) * CAP
    t, z = lax.axis_index("tensor"), lax.axis_index("expert")
    raw = tokens[...]
    values = raw.astype(jnp.float32)
    scale = lax.rsqrt(jnp.mean(values * values, axis=1, keepdims=True) + epsilon)
    normed = (values * scale).astype(jnp.bfloat16)

    expert = lax.broadcasted_iota(jnp.int32, (EXPERTS, tok_count), 0)
    hot = [expert == routes[k : k + 1, :] for k in range(TOP)]
    named = (hot[0] | hot[1]).astype(jnp.bfloat16)
    earlier = (
        lax.broadcasted_iota(jnp.int32, (tok_count, tok_count), 0)
        < lax.broadcasted_iota(jnp.int32, (tok_count, tok_count), 1)
    ).astype(jnp.bfloat16)
    before = jnp.dot(named, earlier, preferred_element_type=jnp.float32)

    row = lax.broadcasted_iota(jnp.int32, (slots, tok_count), 0)
    group = row // CAP
    rank = row - group * CAP
    side = group // (planes + 1)
    plane = group - side * (planes + 1)
    row_expert = 2 * jnp.where(plane == planes, z, jnp.where(plane == z, EXPERTS, plane)) + (t ^ side)
    place = jnp.zeros((slots, tok_count), jnp.float32)
    weight = jnp.zeros((slots, tok_count), jnp.float32)
    for k in range(TOP):
        own_rank = jnp.sum(jnp.where(hot[k], before, 0.0), axis=0, keepdims=True).astype(jnp.int32)
        hit = (row_expert == routes[k : k + 1, :]) & (rank == own_rank)
        place = place + jnp.where(hit, 1.0, 0.0)
        weight = weight + jnp.where(hit, gates[k : k + 1, :], 0.0)
    weights[...] = weight

    rows = jnp.dot(place.astype(jnp.bfloat16), normed, preferred_element_type=jnp.float32).astype(jnp.bfloat16)
    high = weight.astype(jnp.bfloat16)
    low = (weight - high.astype(jnp.float32)).astype(jnp.bfloat16)
    lane = lax.broadcasted_iota(jnp.int32, (LANES, tok_count), 0)
    nt = (((1,), (1,)), ((), ()))
    marks = jnp.zeros((slots, LANES), jnp.float32)
    for part, first in ((high, 0), (low, seqs)):
        member = (lane == seg_row[...] + first).astype(jnp.bfloat16)
        marks = marks + lax.dot_general(part, member, nt, preferred_element_type=jnp.float32)
    marks = marks.astype(jnp.bfloat16)
    start = 0
    for out in (own, own_home, other, other_home):
        stop = start + out.shape[0]
        out[:, :width] = rows[start:stop]
        out[:, width:] = marks[start:stop]
        start = stop

    seq_hot = lax.broadcasted_iota(jnp.int32, (seqs, tok_count), 0) == seg_row[...]
    sums[:, :width] = jnp.dot(seq_hot.astype(jnp.bfloat16), raw, preferred_element_type=jnp.float32)
    counts = jnp.sum(seq_hot.astype(jnp.float32), axis=1, keepdims=True)
    sums[:, width:] = jnp.broadcast_to(counts, (seqs, LANES))


def prep(tokens, routes, gates, segments, seqs, planes):
    tok_count, width = tokens.shape
    vmem = pl.BlockSpec(memory_space=pltpu.VMEM)
    blocks = [
        jax.ShapeDtypeStruct((count * CAP, width + LANES), jnp.bfloat16) for count in (planes, 1, planes, 1)
    ]
    return pl.pallas_call(
        functools.partial(prep_kernel, seqs, planes),
        out_shape=(
            *blocks,
            jax.ShapeDtypeStruct((2 * (planes + 1) * CAP, tok_count), jnp.float32),
            jax.ShapeDtypeStruct((seqs, width + LANES), jnp.float32),
        ),
        in_specs=[vmem] * 4,
        out_specs=(vmem,) * 6,
        name="prep",
    )(tokens, routes.T, gates.T, segments[None, :])


def spans_of(total, tile):
    return [(start, min(tile, total - start)) for start in range(0, total, tile)]


def tie(value, *before):
    return lax.optimization_barrier((value,) + before)[0]


def ffn_kernel(pieces, tile, cols, depth, seqs, pool_in, *refs):
    parts, weights, outs = refs[:pieces], refs[pieces : pieces + 6], refs[pieces + 6 : 2 * pieces + 6]
    pool_out, rows_buf, gate_buf, up_buf, down_buf, hidden, row_sem, in_sem, down_sem = refs[2 * pieces + 6 :]
    t = lax.axis_index("tensor")
    halves = [[w.at[t] for w in weights[:3]], [w.at[t] for w in weights[3:]]]
    size = parts[0].shape[0]
    _, units, width = weights[0].shape
    row_copies = [
        pltpu.make_async_copy(parts[i], rows_buf.at[i, pl.ds(0, size)], row_sem.at[i]) for i in range(pieces)
    ]
    padded = rows_buf.shape[1]
    if padded > size:
        for i in range(pieces):
            rows_buf[i, size:] = jnp.zeros((padded - size, rows_buf.shape[2]), rows_buf.dtype)
    spans = spans_of(units, tile)
    col_spans = spans_of(width, cols)
    copies = []
    for h in range(2):
        for j, (start, length) in enumerate(spans):
            here = pl.ds(start, length)
            copies.append(
                [
                    pltpu.make_async_copy(halves[h][m].at[here], buf.at[h, here], in_sem.at[m, h * len(spans) + j])
                    for m, buf in enumerate((gate_buf, up_buf))
                ]
            )
    for j, (start, length) in enumerate(col_spans):
        here = pl.ds(start, length)
        copies.append(
            [
                pltpu.make_async_copy(
                    halves[h][2].at[:, here], down_buf.at[pl.ds(h * units, units), here], down_sem.at[h, j]
                )
                for h in range(2)
            ]
        )
    for group in copies[:1]:
        for copy in group:
            copy.start()
    for copy in row_copies:
        copy.start()
    for group in copies[1:depth]:
        for copy in group:
            copy.start()

    def arrive(i):
        for copy in copies[i]:
            copy.wait()
        for group in copies[i + depth : i + depth + 1]:
            for copy in group:
                copy.start()

    for copy in row_copies:
        copy.wait()
    x = rows_buf[:, :, :width].reshape(pieces * padded, width)
    marks = rows_buf[:, :, width:].reshape(pieces * padded, LANES).astype(jnp.float32).T[: 2 * seqs].astype(jnp.bfloat16)
    nt = (((1,), (1,)), ((), ()))
    for h in range(2):
        for j, (start, length) in enumerate(spans):
            arrive(h * len(spans) + j)
            here = slice(start, start + length)
            g = lax.dot_general(x, gate_buf[h, here], nt, preferred_element_type=jnp.float32)
            u = lax.dot_general(x, up_buf[h, here], nt, preferred_element_type=jnp.float32)
            value = g / (1.0 + jnp.exp(-g)) * u
            hidden[:, h * units + start : h * units + start + length] = value.astype(jnp.bfloat16)
    pool_out[:, width:] = pool_in[:, width:]
    for j, (start, length) in enumerate(col_spans):
        arrive(2 * len(spans) + j)
        here = slice(start, start + length)
        y = jnp.dot(hidden[...], down_buf[:, here], preferred_element_type=jnp.float32).astype(jnp.bfloat16)
        share = jnp.dot(marks, y, preferred_element_type=jnp.float32)
        pool_out[:, here] = pool_in[:, here] + share[:seqs] + share[seqs:]
        for i in range(pieces):
            outs[i][:, here] = y[i * padded : i * padded + size]


def ffn(parts, weights, pool):
    pieces = len(parts)
    size = parts[0].shape[0]
    _, units, width = weights[0].shape
    tile, cols, depth = 256, 768, 4
    padded = -(-size // 16) * 16
    rows = pieces * padded
    anywhere = pl.BlockSpec(memory_space=pl.ANY)
    vmem = pl.BlockSpec(memory_space=pltpu.VMEM)
    return pl.pallas_call(
        functools.partial(ffn_kernel, pieces, tile, cols, depth, pool.shape[0]),
        out_shape=(jax.ShapeDtypeStruct((size, width), jnp.bfloat16),) * pieces
        + (jax.ShapeDtypeStruct(pool.shape, pool.dtype),),
        in_specs=[vmem] + [anywhere] * (pieces + 6),
        out_specs=(vmem,) * (pieces + 1),
        scratch_shapes=[
            pltpu.VMEM((pieces, padded, width + LANES), jnp.bfloat16),
            pltpu.VMEM((2, units, width), jnp.bfloat16),
            pltpu.VMEM((2, units, width), jnp.bfloat16),
            pltpu.VMEM((2 * units, width), jnp.bfloat16),
            pltpu.VMEM((rows, 2 * units), jnp.bfloat16),
            pltpu.SemaphoreType.DMA((pieces,)),
            pltpu.SemaphoreType.DMA((2, 2 * len(spans_of(units, tile)))),
            pltpu.SemaphoreType.DMA((2, len(spans_of(width, cols)))),
        ],
        compiler_params=pltpu.CompilerParams(vmem_limit_bytes=VMEM_LIMIT),
        cost_estimate=pl.CostEstimate(
            flops=12 * rows * width * units, transcendentals=2 * rows * units, bytes_accessed=12 * units * width
        ),
        name="ffn",
    )(pool, *parts, *weights)


def settle_kernel(planes, *refs):
    parts, out = refs[:-1], refs[-1]
    z = lax.axis_index("expert")
    total = parts[0][...].astype(jnp.float32)
    for part in parts[1:]:
        total = total + part[...].astype(jnp.float32)
    for j in range(planes - 1):
        out[lax.rem(z + 1 + j, planes)] = total[j * CAP : (j + 1) * CAP].astype(jnp.bfloat16)
    out[z] = jnp.zeros(out.shape[1:], jnp.bfloat16)


def settle(parts, planes):
    vmem = pl.BlockSpec(memory_space=pltpu.VMEM)
    return pl.pallas_call(
        functools.partial(settle_kernel, planes),
        out_shape=jax.ShapeDtypeStruct((planes, CAP, parts[0].shape[1]), jnp.bfloat16),
        in_specs=[vmem] * len(parts),
        out_specs=vmem,
        name="settle",
    )(*parts)


def combine_kernel(planes, tokens, weights, early, home, sibling_home, *refs):
    late, out = refs[:-1], refs[-1]
    z = lax.axis_index("expert")
    mixed = jnp.zeros(tokens.shape, jnp.float32)
    half = (planes + 1) * CAP
    parts = [(early, 0), (home, planes * CAP), (sibling_home, half + planes * CAP)]
    for j, part in enumerate(late):
        plane = lax.rem(z + planes - 1 - j, planes)
        parts.append((part, pl.multiple_of(half + plane * CAP, 8)))
    for part, start in parts:
        weight = weights[pl.ds(start, part.shape[0])].T
        high = weight.astype(jnp.bfloat16)
        low = (weight - high.astype(jnp.float32)).astype(jnp.bfloat16)
        for factor in (low, high):
            mixed = mixed + jnp.dot(factor, part[...], preferred_element_type=jnp.float32)
    out[...] = (tokens[...].astype(jnp.float32) + mixed).astype(jnp.bfloat16)


def combine(tokens, weights, early, home, sibling_home, late):
    vmem = pl.BlockSpec(memory_space=pltpu.VMEM)
    return pl.pallas_call(
        functools.partial(combine_kernel, len(late) + 1),
        out_shape=jax.ShapeDtypeStruct(tokens.shape, jnp.bfloat16),
        in_specs=[vmem] * (5 + len(late)),
        out_specs=vmem,
        name="combine",
    )(tokens, weights, early, home, sibling_home, *late)


def added(*arrays):
    total = arrays[0].astype(jnp.float32)
    for array in arrays[1:]:
        total = total + array.astype(jnp.float32)
    return total.astype(jnp.bfloat16)


def core_shards(tokens, routes, gates, segments, w_gate, w_up, w_down):
    tok_count, width = tokens.shape
    chips, cores, planes = (lax.axis_size(name) for name in AXES)
    seqs = tok_count * chips * cores * planes // 256

    own, own_home, other, other_home, weights, pool = prep(tokens, routes, gates, segments, seqs, planes)
    sibling, sibling_home = swap(other, t=1), swap(other_home, t=1)
    stored = (jnp.swapaxes(w_gate, 1, 2), jnp.swapaxes(w_up, 1, 2), w_down)

    tied = lax.optimization_barrier(stored + (sibling, sibling_home))
    far = tuple(pltpu.with_memory_space_constraint(swap(array, t=1), pltpu.HBM) for array in tied[:3])

    z = lax.axis_index("expert")
    others = (planes - 1) * CAP

    def exchange(rows):
        return lax.all_to_all(rows, "expert", split_axis=0, concat_axis=0, tiled=True)

    def turn(block, step):
        return lax.ppermute(block, "expert", [(i, (i + step) % planes) for i in range(planes)])

    def outward(rows):
        return lax.dynamic_slice_in_dim(jnp.concatenate([rows, rows]), (z + 1) * CAP, others)

    def sent_on(arrays):
        return [swap(array, d=step, turned=turned) for array, (step, turned) in zip(arrays, ((1, 2), (2, 1), (3, 3)))]

    def together(arrays, *before):
        return list(lax.optimization_barrier(tuple(arrays) + before))[: len(arrays)]

    home = jnp.concatenate([own_home, sibling_home])
    arrived = exchange(own)
    home_near, home_side = swap(home, d=1, turned=2), swap(home, d=2, turned=1)
    arrived, home_near = together([arrived], home_near)[0], home_near
    early = outward(arrived)
    near, side = swap(early, d=1, turned=2), swap(early, d=2, turned=1)
    late = outward(exchange(tie(sibling, early)))
    first = [early, near, side, swap(near, d=2, turned=1)]
    home = [home, home_near, home_side, swap(home_near, d=2, turned=1)]
    second = [late] + sent_on([late] * 3)

    def back(parts):
        return [parts[0]] + sent_on(parts[1:])

    *partial, pool = ffn(first, stored + far, pool)
    early = back(partial)
    *partial, pool = ffn(second, stored + far, pool)
    early = settle(together(early, pool), planes)
    late = [partial[0]] + sent_on(together(partial[1:], early))
    home[0] = tie(home[0], early)
    early = exchange(early).reshape(planes * CAP, width)
    *partial, pool = ffn(home, stored + far, pool)
    early, *late = together([early] + late, pool)
    late = added(*late)
    partial = together(partial, early)
    home = added(*back(partial))
    late = [turn(late[(j - 1) * CAP : j * CAP], j) for j in range(1, planes)]
    pool = tie(pool, early)
    for axis in ("z", "t", "d"):
        size = lax.axis_size({"t": "tensor", "z": "expert", "d": "dp"}[axis])
        pool = sum([swap(pool, **{axis: step}) for step in range(1, size)], pool)
    late = [swap(block, t=1) for block in late]
    embedded = combine(tokens, weights, early, home[:CAP], swap(home[CAP:], t=1), late)

    pooled = pool[:, :width] / pool[:, width : width + 1]
    return (embedded, pooled)


def slot_numbers(routes):
    flat_routes = routes.reshape(-1)
    pairs = flat_routes.shape[0]
    same = flat_routes[:, None] == flat_routes[None, :]
    earlier = jnp.arange(pairs)[None, :] < jnp.arange(pairs)[:, None]
    slot_rank = jnp.sum((same & earlier).astype(jnp.int32), axis=1)
    return flat_routes * CAP + slot_rank


def shards(tokens, routes, gates, segments, w_gate, w_up, w_down):
    tok_count, width = tokens.shape
    experts_axis = lax.axis_size("expert")
    per_device = w_gate.shape[0]
    replicas = max(1, experts_axis // EXPERTS)
    plane = lax.axis_size("dp") * lax.axis_size("tensor")
    values = tokens.astype(jnp.float32)
    scale = lax.rsqrt(jnp.mean(values * values, axis=1, keepdims=True) + epsilon)
    normed = (values * scale).astype(jnp.bfloat16)
    slot_index = slot_numbers(routes)
    hits = jnp.arange(EXPERTS * CAP, dtype=jnp.int32)[:, None] == slot_index[None, :]
    placing = jnp.sum(hits.astype(jnp.int32).reshape(EXPERTS * CAP, tok_count, TOP), axis=2)
    slot_rows = jnp.dot(placing.astype(jnp.bfloat16), normed, preferred_element_type=jnp.float32)
    shaped = slot_rows.astype(jnp.bfloat16).reshape(EXPERTS, CAP, width)
    if replicas > 1:
        shaped = jnp.repeat(shaped, replicas, axis=0)
    send_rows = shaped.reshape(EXPERTS * replicas * CAP, width)
    received = lax.all_to_all(send_rows, "expert", split_axis=0, concat_axis=0, tiled=True)
    local_rows = received.reshape(experts_axis, per_device, CAP, width)
    block = lax.all_gather(local_rows, ("dp", "tensor"), axis=0, tiled=True)
    gate_proj = jnp.einsum("nacd,adf->nacf", block, w_gate, preferred_element_type=jnp.float32)
    up_proj = jnp.einsum("nacd,adf->nacf", block, w_up, preferred_element_type=jnp.float32)
    hidden = (jax.nn.silu(gate_proj) * up_proj).astype(jnp.bfloat16)
    summed = lax.psum_scatter(
        jnp.einsum("nacf,afd->nacd", hidden, w_down, preferred_element_type=jnp.float32).astype(jnp.bfloat16),
        ("dp", "tensor"),
        scatter_dimension=0,
        tiled=True,
    )
    returned = lax.all_to_all(summed, "expert", split_axis=0, concat_axis=0, tiled=True).astype(jnp.float32)
    expert_out = jnp.sum(returned.reshape(EXPERTS, replicas, CAP, width), axis=1)
    picked = jnp.take(expert_out.reshape(EXPERTS * CAP, width), slot_index, axis=0).reshape(tok_count, TOP, width)
    embedded = (values + jnp.sum(gates[:, :, None] * picked, axis=1)).astype(jnp.bfloat16)
    seq_total = tok_count * plane * experts_axis // 256
    seq_hot = jnp.arange(seq_total, dtype=jnp.int32)[:, None] == segments[None, :]
    seq_sums = jnp.dot(seq_hot.astype(jnp.bfloat16), embedded, preferred_element_type=jnp.float32)
    seq_counts = jnp.sum(seq_hot.astype(jnp.float32), axis=1)
    total_sums, total_counts = lax.psum((seq_sums, seq_counts), AXES)
    return (embedded, total_sums / total_counts[:, None])


def solution(mesh):
    placed = (
        P(AXES, None),
        P(AXES, None),
        P(AXES, None),
        P(AXES),
        P("expert", None, ("dp", "tensor")),
        P("expert", None, ("dp", "tensor")),
        P("expert", ("dp", "tensor"), None),
    )
    dp, tensor, planes = (mesh.shape[name] for name in AXES)
    paired = dp == 4 and tensor == 2 and EXPERTS == tensor * planes and xor_steps(planes)
    return jax.shard_map(
        core_shards if paired else shards,
        mesh=mesh,
        in_specs=placed,
        out_specs=(P(AXES, None), P()),
        check_vma=False,
    )
```
